128 devices in a mesh: blk: 8 (over y, core), row: 16 (over x, z).
Axes of the slice: x: 4, y: 4, z: 4, core: 2. Of those that a mesh axis runs over, the one named last changes fastest.
Arguments:
- factor: float32 [8, 3072, 3072], P('blk', 'row'), may hold values from -1 to 1, as said below
- coupling: float32 [8, 128, 128], P('blk'), may hold values from -1.5 to 1.5
- right_side: float32 [8, 3072, 128], P('blk', 'row'), may hold values from -6 to 6
Outputs:
- inverse: float32 [8, 3072, 3072], P('blk', 'row')
- solution: float32 [8, 3072, 128], P('blk', 'row')
The draws below stay inside these ranges and needn't reach their ends.
Inputs may be any that keep to these rules, and one draw needn't show every extreme that they name: Each factor[b] has ones on its diagonal and zeros above it.
All inputs are finite; a program needn't handle non-finite values.
Results may differ from the reference program's by a relative error of at most 0.0003.
Values sent between devices are 32-bit elements; how exact they have to be, the bound alone decides.
A program may use at most 128 MiB of HBM per device.

```python
import jax
import jax.numpy as jnp
from jax import lax

BW = 128
NRHS = 128
BLOCKS = 8
BLOCK = 3072


def draw_factor(key, part):
    noise = jax.random.normal(key, (BLOCKS, BLOCK, BLOCK), jnp.float32)
    strict = jnp.tril(noise, -1) * BLOCK ** (-0.5)
    return strict + jnp.eye(BLOCK, dtype=jnp.float32)


def block_scale(own_key, extent, shards, least, top_value):
    def one(dim, parts):
        draws = jax.random.uniform(jax.random.fold_in(jax.random.fold_in(own_key, 6), dim), (parts,), jnp.float32, least / len(shards), top_value / len(shards))
        return jnp.repeat(jnp.exp(draws), extent[dim] // parts).reshape((-1,) + (1,) * (len(extent) - dim - 1))

    loudness = one(*shards[0])
    for cut in shards[1:]:
        loudness = loudness * one(*cut)
    return loudness


def normal_values(stream_key, shape, width, reach, pieces=(), held_as=jnp.bfloat16):
    values = width * jax.random.normal(stream_key, shape, jnp.float32)
    if pieces:
        values = values * block_scale(stream_key, shape, pieces, -0.22, 0.18)
    return jnp.clip(values, -reach, reach).astype(held_as)


def setup_inputs(seed: int = 0) -> dict:
    keys = jax.random.split(jax.random.key(seed), 4)
    return {
        "factor": draw_factor(jax.random.fold_in(keys[3], 71), 0),
        "coupling": normal_values(keys[1], (BLOCKS, BW, BW), (max(BW // 9, 1)) ** -0.5, 1.5, ((0, 8),), jnp.float32),
        "right_side": normal_values(keys[2], (BLOCKS, BLOCK, NRHS), 1.0, 6.0, ((0, 8), (1, 16)), jnp.float32),
    }


def invert_block(block_matrix):
    identity = jnp.eye(block_matrix.shape[0], dtype=block_matrix.dtype)
    return jax.scipy.linalg.solve_triangular(block_matrix, identity, lower=True, unit_diagonal=True)

def reference(factor, coupling, right_side):
    inverse = lax.map(invert_block, factor)
    highest = lax.Precision.HIGHEST
    direct = jnp.einsum('nij,njk->nik', inverse, right_side, precision=highest)
    gain_cols = -jnp.einsum('nib,nbc->nic', inverse[:, :, :BW], coupling, precision=highest)

    def forward(tail_rows, items):
        direct_block, gain_block = items
        solved = direct_block + jnp.dot(gain_block, tail_rows, precision=highest)
        return (solved[-BW:], solved)
    start_tail = jnp.zeros((BW, right_side.shape[2]), factor.dtype)
    _, solution = lax.scan(forward, start_tail, (direct, gain_cols))
    return (inverse, solution)
```

```python
import functools

import jax
import jax.numpy as jnp
from jax import lax
from jax.experimental import pallas as pl
from jax.experimental.pallas import tpu as pltpu
from jax.sharding import PartitionSpec as P

MESH = pl.DeviceIdType.MESH
RING = 4
TARGETS = {0: (3, 1, 2), 1: (0, 2), 2: (3,), 3: ()}
RELAYED = {1: (3,)}


def dot(a, b):
    return jnp.dot(a, b, precision=lax.Precision.HIGHEST, preferred_element_type=jnp.float32)


def unit_lower_inverse(matrix):
    size = matrix.shape[0]
    rows = lax.broadcasted_iota(jnp.int32, (size, size), 0)
    cols = lax.broadcasted_iota(jnp.int32, (size, size), 1)
    inverse = jnp.where(rows == cols, 1.0, 0.0).astype(jnp.float32)
    bit = 0
    while (1 << bit) < size:
        same = (rows >> (bit + 1)) == (cols >> (bit + 1))
        corner = same & (((rows >> bit) & 1) == 1) & (((cols >> bit) & 1) == 0)
        below = jnp.where(corner, matrix, 0.0)
        if bit == 0:
            inverse = inverse - below
        else:
            inverse = inverse - dot(dot(inverse, below), inverse)
        bit += 1
    return inverse


class Copies:
    def __init__(self, sems):
        self.sems, self.used, self.ends = sems, 0, []

    def slot(self):
        self.used += 1
        return self.used - 1

    def remote(self, when, source, target, arrival, device, slot=None):
        sem = self.sems.at[self.slot() if slot is None else slot]

        def make():
            return pltpu.make_async_remote_copy(
                src_ref=source,
                dst_ref=target,
                send_sem=sem,
                recv_sem=arrival,
                device_id=device,
                device_id_type=MESH,
            )

        pl.when(when)(lambda: make().start())
        self.ends.append((when, lambda: make().wait_send()))

    def local(self, when, source, target, sem, waited=True):
        pl.when(when)(lambda: pltpu.make_async_copy(source, target, sem).start())
        if waited:
            self.ends.append((when, lambda: pltpu.make_async_copy(source, target, sem).wait()))

    def finish(self):
        for when, end in self.ends:
            pl.when(when)(end)


def arrived(when, target, sem):
    pl.when(when)(lambda: pltpu.make_async_copy(target, target, sem).wait())


def solve_kernel(pairs, fac, diag, corner, rhs, inv, direct, *scratch):
    lbuf = (None, *scratch[: pairs - 1])
    ebuf, own, xa, dinv, dleft, dloc, sends, rl, re, rx, rd, lx = scratch[pairs - 1 :]
    size = fac.shape[0]
    half, wide = size // 2, 2 * size
    blk, row = lax.axis_index("blk"), lax.axis_index("row")
    core = lax.rem(blk, 2)
    x, z = lax.div(row, RING), lax.rem(row, RING)
    zhi, odd = lax.div(z, 2), lax.rem(z, 2)
    mine = 2 * x + zhi
    home = core == 1 - odd
    away = core == odd
    first = blk - core

    def at(to_x, to_z, to_core):
        return {"blk": first + to_core, "row": to_x * RING + to_z}

    def aligned(index, by):
        return pl.multiple_of(index, by)

    barrier = pltpu.get_barrier_semaphore()
    peers = [(x, z, 1 - core)]
    for step in range(1, RING):
        for side in range(2):
            peers += [(x, lax.rem(z + step, RING), side), (lax.rem(x + step, RING), z, side)]
    for peer in peers:
        pl.semaphore_signal(barrier, inc=1, device_id=at(*peer), device_id_type=MESH)
    pl.semaphore_wait(barrier, len(peers))

    copies = Copies(sends)

    def spread(when, source, target, arrival, rows_x, wanted, slots):
        slot = iter(slots)
        for side in range(2):
            src, dst, sem = source(side), target(side), arrival.at[row, side]
            copies.local(when & home, src, dst, sem, waited=False)
            copies.remote(when & home, src, dst, sem, at(x, z, 1 - core), next(slot))
            for r, wx in rows_x:
                for number, to_x in enumerate(TARGETS[r]):
                    copies.remote(
                        when & wx & home, src, dst, sem, at(to_x, z, side), slots[8 + 2 * number + side]
                    )
            across = lax.rem(z + 2, RING)
            copies.remote(
                when & home & wanted(across), src, dst, sem, at(x, across, side), next(slot)
            )
            for step in (1, 3):
                to_z = lax.rem(z + step, RING)
                copies.remote(
                    when & away & wanted(to_z), src, dst, sem, at(x, to_z, side), next(slot)
                )

    def wanted(to_z):
        return (x < RING - 1) | (zhi == 0) | (lax.div(to_z, 2) == 1)

    slots = [copies.slot() for _ in range(14)]
    for m in range(1, pairs):
        spread(
            mine == m,
            lambda side, m=m: fac.at[pl.ds(side * half, half), pl.ds(0, wide * m)],
            lambda side, m=m: lbuf[m].at[pl.ds(aligned(odd * size + side * half, 8), half), :],
            rl,
            [(m // 2, x == m // 2)],
            wanted,
            slots,
        )

    xa[...] = jnp.zeros_like(xa)
    inverse = unit_lower_inverse(diag[...])
    dinv[...] = inverse
    beside = at(x, z + 1 - 2 * odd, core)
    copies.remote(odd == 0, dinv, dleft, rd, beside)
    r_ids = lax.broadcasted_iota(jnp.int32, (size, wide), 0)
    c_ids = lax.broadcasted_iota(jnp.int32, (size, wide), 1)
    place = jnp.where(c_ids == r_ids + odd * size, 1.0, 0.0).astype(jnp.float32)
    own[:, pl.ds(0, wide)] = dot(inverse, place)
    own[:, pl.ds(wide, rhs.shape[1])] = rhs[...]

    @pl.when(odd == 1)
    def _():
        pltpu.make_async_copy(dleft, dleft, rd).wait()
        left = dot(dinv[...], dot(corner[...], dleft[...]))
        lead = jnp.where(c_ids == r_ids, 1.0, 0.0).astype(jnp.float32)
        own[:, pl.ds(0, wide)] = own[:, pl.ds(0, wide)] - dot(left, lead)

    slots = [copies.slot() for _ in range(14)]
    spread(
        mine >= 0,
        lambda side: own.at[pl.ds(side * half, half), :],
        lambda side: ebuf.at[pl.ds(aligned(row * size + side * half, 8), half), :],
        re,
        [(r, x == r) for r in range(RING)],
        wanted,
        slots,
    )

    def view(kind, j, side):
        if kind == "left":
            return lbuf[j // 2].at[pl.ds(aligned((j % 2) * size + side * half, 8), half), :]
        return ebuf.at[pl.ds(aligned(j * size + side * half, 8), half), :]

    def sem_of(kind, j, side):
        return (rl if kind == "left" else re).at[j, side]

    def panels(kind, numbers):
        return [j for j in numbers if kind == "right" or j >= 2]

    def forward(kind, j, when, targets, beside_too):
        here, sem = view(kind, j, core), sem_of(kind, j, core)
        arrived(when, here, sem)
        for to_x in targets:
            copies.remote(when, here, here, sem, at(to_x, z, core))
        if beside_too is not None:
            copies.remote(when & beside_too, here, here, sem, at(x, z, 1 - core))

    for kind in ("left", "right"):
        for r in range(RING):
            for j in panels(kind, range(RING * r, RING * (r + 1))):
                when = (x == r) & (z != j % RING)
                if r == RING - 1 and j % RING >= 2:
                    when = when & (zhi == 1)
                forward(kind, j, when, TARGETS[r], mine >= j // 2)
    for kind in ("left", "right"):
        for r, targets in RELAYED.items():
            for j in panels(kind, range(RING * r, RING * (r + 1))):
                forward(kind, j, x == 0, targets, None)

    def take(m):
        for kind in ("left", "right"):
            for j in panels(kind, (2 * m, 2 * m + 1)):
                forward(kind, j, x > m // 2, (), mine >= 0)

    partner = at(x, z + 1 - 2 * odd, 1 - core)
    half_of_pair = jnp.where(home, odd, 1 - odd)

    def solve(m):
        here = mine >= m
        for kind in ("left", "right"):
            for j in panels(kind, (2 * m, 2 * m + 1)):
                arrived(row == j, view(kind, j, core), sem_of(kind, j, core))
                arrived(here, view(kind, j, 1 - core), sem_of(kind, j, 1 - core))
        block = xa.at[:, pl.ds(m * wide, wide)]

        @pl.when(mine == m)
        def _():
            block[...] = ebuf[pl.ds(aligned(m * wide + half_of_pair * size, 8), size), pl.ds(0, wide)]

        @pl.when(mine > m)
        def _():
            block[...] = dot(block[...], ebuf[pl.ds(m * wide, wide), pl.ds(0, wide)])

        @pl.when(here)
        def _():
            dloc[...] += dot(block[...], ebuf[pl.ds(m * wide, wide), pl.ds(wide, dloc.shape[1])])

        if m:

            @pl.when(here)
            def _():
                @pl.loop(0, m)
                def _(n):
                    cols = pl.ds(pl.multiple_of(n * wide, wide), wide)
                    xa[:, cols] -= dot(block[...], lbuf[m][:, cols])

        result = inv.at[:, pl.ds(m * wide, wide)]
        copies.local((mine < m) | home, block, result, lx.at[m])
        copies.remote(here & away, block, result, rx.at[m], partner)

    dloc[...] = jnp.zeros_like(dloc)
    for m in reversed(range(pairs)):
        solve(m)
        if 2 <= m:
            take(m - 2)
    copies.local(home, dloc, direct, lx.at[pairs])
    copies.remote(away, dloc, direct, rx.at[pairs], partner)

    for m in range(pairs):
        arrived(away & (mine >= m), inv.at[:, pl.ds(m * wide, wide)], rx.at[m])
    arrived(away, direct, rx.at[pairs])
    copies.finish()


def invert(factor, right_side):
    size, order = factor.shape
    columns = right_side.shape[1]
    pairs, wide = order // (2 * size), 2 * size
    row = lax.axis_index("row")
    diag = lax.dynamic_slice_in_dim(factor, row * size, size, 1)
    corner = lax.dynamic_slice_in_dim(factor, (row - row % 2) * size, size, 1)
    vmem = pl.BlockSpec(memory_space=pltpu.VMEM)
    hbm = pl.BlockSpec(memory_space=pl.ANY)
    dma = pltpu.SemaphoreType.DMA
    panels = 2 * pairs
    return pl.pallas_call(
        functools.partial(solve_kernel, pairs),
        out_shape=(
            jax.ShapeDtypeStruct((size, order), jnp.float32),
            jax.ShapeDtypeStruct((size, columns), jnp.float32),
        ),
        in_specs=[vmem] * 4,
        out_specs=(hbm, hbm),
        scratch_shapes=[
            *[pltpu.VMEM((wide, wide * m), jnp.float32) for m in range(1, pairs)],
            pltpu.VMEM((order, wide + columns), jnp.float32),
            pltpu.VMEM((size, wide + columns), jnp.float32),
            pltpu.VMEM((size, order), jnp.float32),
            pltpu.VMEM((size, size), jnp.float32),
            pltpu.VMEM((size, size), jnp.float32),
            pltpu.VMEM((size, columns), jnp.float32),
            dma((200,)),
            dma((panels, 2)),
            dma((panels, 2)),
            dma((pairs + 1,)),
            dma,
            dma((pairs + 1,)),
        ],
        compiler_params=pltpu.CompilerParams(
            collective_id=0, has_side_effects=True, vmem_limit_bytes=52 * 1024 * 1024
        ),
    )(factor, diag, corner, right_side)


def tail_kernel(inv, direct, coupling, out, lead, gain, mapped, maps, tail, sends, rm, rt, lsem):
    size, width = lead.shape
    blocks, rows = maps.shape[0], lax.axis_size("row")
    blk, row = lax.axis_index("blk"), lax.axis_index("row")
    last = row == rows - 1
    barrier = pltpu.get_barrier_semaphore()

    def greet(when, device):
        def _():
            pl.semaphore_signal(barrier, inc=1, device_id=device, device_id_type=MESH)

        pl.when(when)(_)

    others = [{"blk": lax.rem(blk + step, blocks), "row": row} for step in range(1, blocks)]
    along = [{"blk": blk, "row": number} for number in range(rows - 1)]
    for device in others + along:
        greet(last, device)
    greet(row != rows - 1, {"blk": blk, "row": rows - 1})
    pl.when(last)(lambda: pl.semaphore_wait(barrier, blocks + rows - 2))
    pl.when(row != rows - 1)(lambda: pl.semaphore_wait(barrier, 1))

    copies = Copies(sends)
    fetch = pltpu.make_async_copy(inv.at[:, pl.ds(0, width)], lead, lsem)
    fetch.start()
    fetch.wait()
    gain[...] = -dot(lead[...], coupling[...])

    @pl.when(last | (blk == 0))
    def _():
        tail[...] = jnp.zeros_like(tail)

    @pl.when(last)
    def _():
        mapped[:, pl.ds(0, width)] = gain[pl.ds(size - width, width), :]
        mapped[:, pl.ds(width, direct.shape[1])] = direct[pl.ds(size - width, width), :]

    for step in range(1, blocks):
        copies.remote(
            last & (blk + step < blocks),
            mapped,
            maps.at[blk],
            rm.at[blk],
            {"blk": lax.rem(blk + step, blocks), "row": row},
        )
    for k in range(blocks - 1):

        @pl.when(last & (blk > k))
        def _():
            pltpu.make_async_copy(maps.at[k], maps.at[k], rm.at[k]).wait()
            tail[...] = (
                dot(maps[k, :, pl.ds(0, width)], tail[...])
                + maps[k, :, pl.ds(width, tail.shape[1])]
            )

    for device in along:
        copies.remote(last & (blk > 0), tail, tail, rt, device)
    arrived((row != rows - 1) & (blk > 0), tail, rt)
    out[...] = direct[...] + dot(gain[...], tail[...])
    copies.finish()


def chain(inverse, direct, coupling):
    size, columns = direct.shape
    width = coupling.shape[0]
    blocks, rows = lax.axis_size("blk"), lax.axis_size("row")
    vmem = pl.BlockSpec(memory_space=pltpu.VMEM)
    dma = pltpu.SemaphoreType.DMA
    return pl.pallas_call(
        tail_kernel,
        out_shape=jax.ShapeDtypeStruct((size, columns), jnp.float32),
        in_specs=[pl.BlockSpec(memory_space=pl.ANY), vmem, vmem],
        out_specs=vmem,
        scratch_shapes=[
            pltpu.VMEM((size, width), jnp.float32),
            pltpu.VMEM((size, width), jnp.float32),
            pltpu.VMEM((width, width + columns), jnp.float32),
            pltpu.VMEM((blocks, width, width + columns), jnp.float32),
            pltpu.VMEM((width, columns), jnp.float32),
            dma((blocks + rows,)),
            dma((blocks,)),
            dma,
            dma,
        ],
        compiler_params=pltpu.CompilerParams(
            collective_id=1, has_side_effects=True, vmem_limit_bytes=16 * 1024 * 1024
        ),
    )(inverse, direct, coupling)


def on_device(factor, coupling, right_side):
    inverse, direct = invert(factor[0], right_side[0])
    return inverse[None], chain(inverse, direct, coupling[0])[None]


def solution(mesh):
    in_specs = (P("blk", "row", None), P("blk", None, None), P("blk", "row", None))
    out_specs = (P("blk", "row", None), P("blk", "row", None))
    return jax.shard_map(
        on_device, mesh=mesh, in_specs=in_specs, out_specs=out_specs, check_vma=False
    )
```

```python
import functools

import jax
import jax.numpy as jnp
from jax import lax
from jax.experimental import pallas as pl
from jax.experimental.pallas import tpu as pltpu
from jax.sharding import PartitionSpec as P

MESH = pl.DeviceIdType.MESH
RING = 4
TARGETS = {0: (3, 1, 2), 1: (0, 2), 2: (3,), 3: ()}
RELAYED = {1: (3,)}


def dot(a, b):
    return jnp.dot(a, b, precision=lax.Precision.HIGHEST, preferred_element_type=jnp.float32)


def split(a):
    high = a.astype(jnp.bfloat16)
    return high, (a - high.astype(jnp.float32)).astype(jnp.bfloat16)


def dot3(a, b):
    (a_high, a_low), (b_high, b_low) = a, b

    def one(p, q):
        return jnp.dot(p, q, preferred_element_type=jnp.float32)

    return one(a_high, b_high) + (one(a_high, b_low) + one(a_low, b_high))


def unit_lower_inverse(matrix):
    size = matrix.shape[0]
    rows = lax.broadcasted_iota(jnp.int32, (size, size), 0)
    cols = lax.broadcasted_iota(jnp.int32, (size, size), 1)
    inverse = jnp.where(rows == cols, 1.0, 0.0).astype(jnp.float32)
    bit = 0
    while (1 << bit) < size:
        same = (rows >> (bit + 1)) == (cols >> (bit + 1))
        corner = same & (((rows >> bit) & 1) == 1) & (((cols >> bit) & 1) == 0)
        below = jnp.where(corner, matrix, 0.0)
        if bit == 0:
            inverse = inverse - below
        else:
            inverse = inverse - dot(dot(inverse, below), inverse)
        bit += 1
    return inverse


class Copies:
    def __init__(self, sems):
        self.sems, self.used, self.groups, self.depth, self.ending = sems, 0, [], 0, False

    def slot(self):
        self.used += 1
        return self.used - 1

    def group(self, when, body):
        if not self.depth and not self.ending:
            self.groups.append((when, body, self.used))
        self.depth += 1
        pl.when(when)(lambda: body())
        self.depth -= 1

    def arrived(self, target, sem):
        if not self.ending:
            pltpu.make_async_copy(target, target, sem).wait()

    def remote(self, source, target, arrival, device, slot=None):
        copy = pltpu.make_async_remote_copy(
            src_ref=source,
            dst_ref=target,
            send_sem=self.sems.at[self.slot() if slot is None else slot],
            recv_sem=arrival,
            device_id=device,
            device_id_type=MESH,
        )
        if self.ending:
            copy.wait_send()
        else:
            copy.start()

    def local(self, source, target, sem, waited=True):
        copy = pltpu.make_async_copy(source, target, sem)
        if not self.ending:
            copy.start()
        elif waited:
            copy.wait()

    def finish(self):
        self.ending = True
        for when, body, self.used in self.groups:
            self.group(when, body)


def solve_kernel(pairs, fac, diag, corner, rhs, inv, direct, *scratch):
    lbuf = (None, *scratch[: pairs - 1])
    ebuf, own, xa, dinv, dleft, dloc, parts, sends, rl, re, rx, rd, lx = scratch[pairs - 1 :]
    size = fac.shape[0]
    half, wide = size // 2, 2 * size
    blk, row = lax.axis_index("blk"), lax.axis_index("row")
    core = lax.rem(blk, 2)
    x, z = lax.div(row, RING), lax.rem(row, RING)
    zhi, odd = lax.div(z, 2), lax.rem(z, 2)
    mine = 2 * x + zhi
    home = core == 1 - odd
    away = core == odd
    first = blk - core

    def at(to_x, to_z, to_core):
        return {"blk": first + to_core, "row": to_x * RING + to_z}

    def aligned(index, by):
        return pl.multiple_of(index, by)

    barrier = pltpu.get_barrier_semaphore()
    peers = [(x, z, 1 - core)]
    for step in range(1, RING):
        for side in range(2):
            peers += [(x, lax.rem(z + step, RING), side), (lax.rem(x + step, RING), z, side)]
    for peer in peers:
        pl.semaphore_signal(barrier, inc=1, device_id=at(*peer), device_id_type=MESH)

    xa[...] = jnp.zeros_like(xa)
    dloc[...] = jnp.zeros_like(dloc)
    dinv[...] = unit_lower_inverse(diag[...])
    pl.semaphore_wait(barrier, len(peers))

    copies = Copies(sends)
    beside = at(x, z + 1 - 2 * odd, core)
    copies.group(odd == 0, lambda: copies.remote(dinv, dleft, rd, beside))

    def near(source, target, arrival, slots):
        sides = [(source(side), target(side), arrival.at[row, side], side) for side in range(2)]

        def at_home():
            for src, dst, sem, side in sides:
                copies.remote(src, dst, sem, at(x, z, 1 - core), slots[side])
                copies.local(src, dst, sem, waited=False)

        def along(targets):
            for number, to_x in enumerate(targets):
                for src, dst, sem, side in sides:
                    copies.remote(src, dst, sem, at(to_x, z, side), slots[2 * number + 2 + side])

        copies.group(home, at_home)
        for r, targets in TARGETS.items():
            if targets:
                copies.group(home & (x == r), functools.partial(along, targets))
        for number, step in enumerate((1, 3)):
            to_z = lax.rem(z + step, RING)

            def beside(number=number, to_z=to_z):
                for src, dst, sem, side in sides:
                    copies.remote(src, dst, sem, at(x, to_z, side), slots[2 * number + side])

            copies.group(away & wanted(to_z), beside)

    def far(source, target, arrival, slots):
        to_z = lax.rem(z + 2, RING)

        def across():
            for side in range(2):
                copies.remote(
                    source(side), target(side), arrival.at[row, side], at(x, to_z, side), slots[side]
                )

        copies.group(home & wanted(to_z), across)

    def wanted(to_z):
        return (x < RING - 1) | (zhi == 0) | (lax.div(to_z, 2) == 1)

    def own_left(how, slots, numbers):
        for m in numbers:
            if m == 0:
                continue
            copies.group(
                mine == m,
                lambda m=m: how(
                    lambda side: fac.at[pl.ds(side * half, half), pl.ds(0, wide * m)],
                    lambda side: lbuf[m].at[pl.ds(aligned(odd * size + side * half, 8), half), :],
                    rl,
                    slots,
                ),
            )

    def own_right(how, slots):
        how(
            lambda side: own.at[pl.ds(side * half, half), :],
            lambda side: ebuf.at[pl.ds(aligned(row * size + side * half, 8), half), :],
            re,
            slots,
        )

    slots = [copies.slot() for _ in range(8)]
    own_left(near, slots, range(pairs))
    farther = [copies.slot() for _ in range(4)]

    r_ids = lax.broadcasted_iota(jnp.int32, (size, wide), 0)
    c_ids = lax.broadcasted_iota(jnp.int32, (size, wide), 1)
    place = jnp.where(c_ids == r_ids + odd * size, 1.0, 0.0).astype(jnp.float32)
    own[:, pl.ds(0, wide)] = dot(dinv[...], place)
    own[:, pl.ds(wide, rhs.shape[1])] = rhs[...]

    @pl.when(odd == 1)
    def _():
        pltpu.make_async_copy(dleft, dleft, rd).wait()
        left = dot(dinv[...], dot(corner[...], dleft[...]))
        lead = jnp.where(c_ids == r_ids, 1.0, 0.0).astype(jnp.float32)
        own[:, pl.ds(0, wide)] = own[:, pl.ds(0, wide)] - dot(left, lead)

    slots = [copies.slot() for _ in range(8)]
    own_right(near, slots)

    def view(kind, j, side):
        if kind == "left":
            return lbuf[j // 2].at[pl.ds(aligned((j % 2) * size + side * half, 8), half), :]
        return ebuf.at[pl.ds(aligned(j * size + side * half, 8), half), :]

    def sem_of(kind, j, side):
        return (rl if kind == "left" else re).at[j, side]

    def panels(kind, numbers):
        return [j for j in numbers if kind == "right" or j >= 2]

    def forward(kind, j, when, targets, beside_too):
        here, sem = view(kind, j, core), sem_of(kind, j, core)

        def pass_on():
            copies.arrived(here, sem)
            for to_x in targets:
                copies.remote(here, here, sem, at(to_x, z, core))
            if beside_too is not None:
                copies.group(
                    beside_too, lambda: copies.remote(here, here, sem, at(x, z, 1 - core))
                )

        copies.group(when, pass_on)

    def row_pass(kind, r, hops, targets, beside_too=True):
        for j in panels(kind, range(RING * r, RING * (r + 1))):
            apart = lax.rem(z + RING - j % RING, RING)
            when = lax.rem(apart, 2) == 1 if hops == 1 else apart == hops
            if r == RING - 1 and j % RING >= 2:
                when = when & (zhi == 1)
            forward(kind, j, when, targets, (mine >= j // 2) if beside_too else None)

    for r in range(RING):

        def own_row(r=r):
            relays = [(kind, q, RELAYED[q]) for q in RELAYED for kind in ("left", "right") if r == 0]

            def relay(kind, hops):
                for name, q, targets in relays:
                    if name == kind:
                        row_pass(kind, q, hops, targets, False)

            row_pass("left", r, 1, TARGETS[r])
            own_left(far, farther[:2], (2 * r, 2 * r + 1))
            relay("left", 0)
            row_pass("right", r, 1, TARGETS[r])
            own_right(far, farther[2:])
            relay("left", 1)
            row_pass("left", r, 2, TARGETS[r])
            row_pass("right", r, 2, TARGETS[r])
            relay("left", 2)
            for hops in range(3):
                relay("right", hops)

        copies.group(x == r, own_row)

    def take(m):
        def body():
            for kind in ("left", "right"):
                for j in panels(kind, (2 * m, 2 * m + 1)):
                    forward(kind, j, True, (), True)

        copies.group(x > m // 2, body)

    partner = at(x, z + 1 - 2 * odd, 1 - core)
    half_of_pair = jnp.where(home, odd, 1 - odd)

    def solve(m):
        here = mine >= m

        def wait():
            for kind in ("left", "right"):
                for j in panels(kind, (2 * m, 2 * m + 1)):
                    pl.when(row == j)(
                        lambda kind=kind, j=j: copies.arrived(view(kind, j, core), sem_of(kind, j, core))
                    )
                    copies.arrived(view(kind, j, 1 - core), sem_of(kind, j, 1 - core))

        pl.when(here)(wait)
        block = xa.at[:, pl.ds(m * wide, wide)]

        @pl.when(mine == m)
        def _():
            block[...] = ebuf[pl.ds(aligned(m * wide + half_of_pair * size, 8), size), pl.ds(0, wide)]

        @pl.when(mine > m)
        def _():
            block[...] = dot3(split(block[...]), split(ebuf[pl.ds(m * wide, wide), pl.ds(0, wide)]))

        @pl.when(here)
        def _():
            solved = split(block[...])
            dloc[...] += dot3(
                solved, split(ebuf[pl.ds(m * wide, wide), pl.ds(wide, dloc.shape[1])])
            )
            parts[0, :, :], parts[1, :, :] = solved
            if m:

                @pl.loop(0, m)
                def _(n):
                    cols = pl.ds(pl.multiple_of(n * wide, wide), wide)
                    xa[:, cols] -= dot3((parts[0], parts[1]), split(lbuf[m][:, cols]))

        result = inv.at[:, pl.ds(m * wide, wide)]
        copies.group((mine < m) | home, lambda: copies.local(block, result, lx.at[m]))
        copies.group(here & away, lambda: copies.remote(block, result, rx.at[m], partner))

    for m in reversed(range(pairs)):
        solve(m)
        if 2 <= m:
            take(m - 2)
    copies.group(home, lambda: copies.local(dloc, direct, lx.at[pairs]))
    copies.group(away, lambda: copies.remote(dloc, direct, rx.at[pairs], partner))

    @pl.when(away)
    def _():
        for m in range(pairs):
            result = inv.at[:, pl.ds(m * wide, wide)]
            pl.when(mine >= m)(lambda m=m, result=result: copies.arrived(result, rx.at[m]))
        copies.arrived(direct, rx.at[pairs])

    copies.finish()


def invert(factor, right_side):
    size, order = factor.shape
    columns = right_side.shape[1]
    pairs, wide = order // (2 * size), 2 * size
    row = lax.axis_index("row")
    diag = lax.dynamic_slice_in_dim(factor, row * size, size, 1)
    corner = lax.dynamic_slice_in_dim(factor, (row - row % 2) * size, size, 1)
    vmem = pl.BlockSpec(memory_space=pltpu.VMEM)
    hbm = pl.BlockSpec(memory_space=pl.ANY)
    dma = pltpu.SemaphoreType.DMA
    panels = 2 * pairs
    return pl.pallas_call(
        functools.partial(solve_kernel, pairs),
        out_shape=(
            jax.ShapeDtypeStruct((size, order), jnp.float32),
            jax.ShapeDtypeStruct((size, columns), jnp.float32),
        ),
        in_specs=[vmem] * 4,
        out_specs=(hbm, hbm),
        scratch_shapes=[
            *[pltpu.VMEM((wide, wide * m), jnp.float32) for m in range(1, pairs)],
            pltpu.VMEM((order, wide + columns), jnp.float32),
            pltpu.VMEM((size, wide + columns), jnp.float32),
            pltpu.VMEM((size, order), jnp.float32),
            pltpu.VMEM((size, size), jnp.float32),
            pltpu.VMEM((size, size), jnp.float32),
            pltpu.VMEM((size, columns), jnp.float32),
            pltpu.VMEM((2, size, wide), jnp.bfloat16),
            dma((400,)),
            dma((panels, 2)),
            dma((panels, 2)),
            dma((pairs + 1,)),
            dma,
            dma((pairs + 1,)),
        ],
        compiler_params=pltpu.CompilerParams(
            collective_id=0, has_side_effects=True, vmem_limit_bytes=52 * 1024 * 1024
        ),
    )(factor, diag, corner, right_side)


def tail_kernel(inv, direct, coupling, out, lead, gain, mapped, maps, tail, sends, rm, rt, lsem):
    size, width = lead.shape
    blocks, rows = maps.shape[0], lax.axis_size("row")
    blk, row = lax.axis_index("blk"), lax.axis_index("row")
    last = row == rows - 1
    barrier = pltpu.get_barrier_semaphore()

    def greet(when, device):
        def _():
            pl.semaphore_signal(barrier, inc=1, device_id=device, device_id_type=MESH)

        pl.when(when)(_)

    others = [{"blk": lax.rem(blk + step, blocks), "row": row} for step in range(1, blocks)]
    along = [{"blk": blk, "row": number} for number in range(rows - 1)]
    for device in others + along:
        greet(last, device)
    greet(row != rows - 1, {"blk": blk, "row": rows - 1})
    pl.when(last)(lambda: pl.semaphore_wait(barrier, blocks + rows - 2))
    pl.when(row != rows - 1)(lambda: pl.semaphore_wait(barrier, 1))

    copies = Copies(sends)
    fetch = pltpu.make_async_copy(inv.at[:, pl.ds(0, width)], lead, lsem)
    fetch.start()
    fetch.wait()
    gain[...] = -dot(lead[...], coupling[...])

    @pl.when(last | (blk == 0))
    def _():
        tail[...] = jnp.zeros_like(tail)

    @pl.when(last)
    def _():
        mapped[:, pl.ds(0, width)] = gain[pl.ds(size - width, width), :]
        mapped[:, pl.ds(width, direct.shape[1])] = direct[pl.ds(size - width, width), :]

    for step in range(1, blocks):
        later = {"blk": lax.rem(blk + step, blocks), "row": row}
        copies.group(
            last & (blk + step < blocks),
            lambda later=later: copies.remote(mapped, maps.at[blk], rm.at[blk], later),
        )
    for k in range(blocks - 1):

        @pl.when(last & (blk > k))
        def _():
            pltpu.make_async_copy(maps.at[k], maps.at[k], rm.at[k]).wait()
            tail[...] = (
                dot(maps[k, :, pl.ds(0, width)], tail[...])
                + maps[k, :, pl.ds(width, tail.shape[1])]
            )

    def hand_out():
        for device in along:
            copies.remote(tail, tail, rt, device)

    copies.group(last & (blk > 0), hand_out)
    pl.when((row != rows - 1) & (blk > 0))(lambda: copies.arrived(tail, rt))
    out[...] = direct[...] + dot(gain[...], tail[...])
    copies.finish()


def chain(inverse, direct, coupling):
    size, columns = direct.shape
    width = coupling.shape[0]
    blocks, rows = lax.axis_size("blk"), lax.axis_size("row")
    vmem = pl.BlockSpec(memory_space=pltpu.VMEM)
    dma = pltpu.SemaphoreType.DMA
    return pl.pallas_call(
        tail_kernel,
        out_shape=jax.ShapeDtypeStruct((size, columns), jnp.float32),
        in_specs=[pl.BlockSpec(memory_space=pl.ANY), vmem, vmem],
        out_specs=vmem,
        scratch_shapes=[
            pltpu.VMEM((size, width), jnp.float32),
            pltpu.VMEM((size, width), jnp.float32),
            pltpu.VMEM((width, width + columns), jnp.float32),
            pltpu.VMEM((blocks, width, width + columns), jnp.float32),
            pltpu.VMEM((width, columns), jnp.float32),
            dma((blocks + rows,)),
            dma((blocks,)),
            dma,
            dma,
        ],
        compiler_params=pltpu.CompilerParams(
            collective_id=1, has_side_effects=True, vmem_limit_bytes=16 * 1024 * 1024
        ),
    )(inverse, direct, coupling)


def on_device(factor, coupling, right_side):
    inverse, direct = invert(factor[0], right_side[0])
    return inverse[None], chain(inverse, direct, coupling[0])[None]


def solution(mesh):
    in_specs = (P("blk", "row", None), P("blk", None, None), P("blk", "row", None))
    out_specs = (P("blk", "row", None), P("blk", "row", None))
    return jax.shard_map(
        on_device, mesh=mesh, in_specs=in_specs, out_specs=out_specs, check_vma=False
    )
```

```python
import functools

import jax
import jax.numpy as jnp
from jax import lax
from jax.experimental import pallas as pl
from jax.experimental.pallas import tpu as pltpu
from jax.sharding import PartitionSpec as P

MESH = pl.DeviceIdType.MESH
RING = 4
TARGETS = {0: (3, 1, 2), 1: (0, 2), 2: (3,), 3: ()}
RELAYED = {1: (3,)}


def dot(a, b):
    return jnp.dot(a, b, precision=lax.Precision.HIGHEST, preferred_element_type=jnp.float32)


def split(a):
    high = a.astype(jnp.bfloat16)
    return high, (a - high.astype(jnp.float32)).astype(jnp.bfloat16)


def dot3(a, b):
    (a_high, a_low), (b_high, b_low) = a, b

    def one(p, q):
        return jnp.dot(p, q, preferred_element_type=jnp.float32)

    return one(a_high, b_high) + (one(a_high, b_low) + one(a_low, b_high))


def unit_lower_inverse(matrix):
    size = matrix.shape[0]
    rows = lax.broadcasted_iota(jnp.int32, (size, size), 0)
    cols = lax.broadcasted_iota(jnp.int32, (size, size), 1)
    inverse = jnp.where(rows == cols, 1.0, 0.0).astype(jnp.float32)
    bit = 0
    while (1 << bit) < size:
        same = (rows >> (bit + 1)) == (cols >> (bit + 1))
        corner = same & (((rows >> bit) & 1) == 1) & (((cols >> bit) & 1) == 0)
        below = jnp.where(corner, matrix, 0.0)
        if bit == 0:
            inverse = inverse - below
        else:
            inverse = inverse - dot(dot(inverse, below), inverse)
        bit += 1
    return inverse


class Copies:
    def __init__(self, sems):
        self.sems, self.used, self.groups, self.depth, self.ending = sems, 0, [], 0, False

    def slot(self):
        self.used += 1
        return self.used - 1

    def group(self, when, body):
        if not self.depth and not self.ending:
            self.groups.append((when, body, self.used))
        self.depth += 1
        pl.when(when)(lambda: body())
        self.depth -= 1

    def arrived(self, target, sem):
        if not self.ending:
            pltpu.make_async_copy(target, target, sem).wait()

    def remote(self, source, target, arrival, device, slot=None):
        copy = pltpu.make_async_remote_copy(
            src_ref=source,
            dst_ref=target,
            send_sem=self.sems.at[self.slot() if slot is None else slot],
            recv_sem=arrival,
            device_id=device,
            device_id_type=MESH,
        )
        if self.ending:
            copy.wait_send()
        else:
            copy.start()

    def local(self, source, target, sem, waited=True):
        copy = pltpu.make_async_copy(source, target, sem)
        if not self.ending:
            copy.start()
        elif waited:
            copy.wait()

    def finish(self):
        self.ending = True
        for when, body, self.used in self.groups:
            self.group(when, body)


def solve_kernel(pairs, planes, fac, diag, corner, rhs, coupling, inv, solved, *scratch):
    lbuf = (None, *scratch[: pairs - 1])
    ebuf, own, xa, dinv, dleft, dloc, parts, cpl, gain, maps, mine_map, joined, tail = scratch[
        pairs - 1 : pairs + 12
    ]
    sends, rl, re, rx, rd, lx, rc, rp, rj, rt = scratch[pairs + 12 :]
    size = fac.shape[0]
    half, wide = size // 2, 2 * size
    blk, row = lax.axis_index("blk"), lax.axis_index("row")
    core = lax.rem(blk, 2)
    x, z = lax.div(row, RING), lax.rem(row, RING)
    zhi, odd = lax.div(z, 2), lax.rem(z, 2)
    mine = 2 * x + zhi
    home = core == 1 - odd
    away = core == odd
    first = blk - core

    def at(to_x, to_z, to_core):
        return {"blk": first + to_core, "row": to_x * RING + to_z}

    def aligned(index, by):
        return pl.multiple_of(index, by)

    barrier = pltpu.get_barrier_semaphore()
    peers = [(x, z, 1 - core)]
    for step in range(1, RING):
        for side in range(2):
            peers += [(x, lax.rem(z + step, RING), side), (lax.rem(x + step, RING), z, side)]
    others = [
        {"blk": lax.rem(blk + 2 * step, 2 * planes), "row": row} for step in range(1, planes)
    ]
    peers = [at(*peer) for peer in peers] + others
    for peer in peers:
        pl.semaphore_signal(barrier, inc=1, device_id=peer, device_id_type=MESH)

    xa[...] = jnp.zeros_like(xa)
    dloc[...] = jnp.zeros_like(dloc)
    dinv[...] = unit_lower_inverse(diag[...])
    pl.semaphore_wait(barrier, len(peers))

    copies = Copies(sends)
    beside = at(x, z + 1 - 2 * odd, core)

    def share_coupling():
        copies.local(coupling, cpl, rc, waited=False)
        copies.remote(coupling, cpl, rc, at(x, z, 1 - core))

    copies.group(home, share_coupling)
    copies.group(odd == 0, lambda: copies.remote(dinv, dleft, rd, beside))

    def near(source, target, arrival, slots):
        sides = [(source(side), target(side), arrival.at[row, side], side) for side in range(2)]

        def at_home():
            for src, dst, sem, side in sides:
                copies.remote(src, dst, sem, at(x, z, 1 - core), slots[side])
                copies.local(src, dst, sem, waited=False)

        def along(targets):
            for number, to_x in enumerate(targets):
                for src, dst, sem, side in sides:
                    copies.remote(src, dst, sem, at(to_x, z, side), slots[2 * number + 2 + side])

        copies.group(home, at_home)
        for r, targets in TARGETS.items():
            if targets:
                copies.group(home & (x == r), functools.partial(along, targets))
        for number, step in enumerate((1, 3)):
            to_z = lax.rem(z + step, RING)

            def beside(number=number, to_z=to_z):
                for src, dst, sem, side in sides:
                    copies.remote(src, dst, sem, at(x, to_z, side), slots[2 * number + side])

            copies.group(away & wanted(to_z), beside)

    def far(source, target, arrival, slots):
        to_z = lax.rem(z + 2, RING)

        def across():
            for side in range(2):
                copies.remote(
                    source(side), target(side), arrival.at[row, side], at(x, to_z, side), slots[side]
                )

        copies.group(home & wanted(to_z), across)

    def wanted(to_z):
        return (x < RING - 1) | (zhi == 0) | (lax.div(to_z, 2) == 1)

    def own_left(how, slots, numbers):
        for m in numbers:
            if m == 0:
                continue
            copies.group(
                mine == m,
                lambda m=m: how(
                    lambda side: fac.at[pl.ds(side * half, half), pl.ds(0, wide * m)],
                    lambda side: lbuf[m].at[pl.ds(aligned(odd * size + side * half, 8), half), :],
                    rl,
                    slots,
                ),
            )

    def own_right(how, slots):
        how(
            lambda side: own.at[pl.ds(side * half, half), :],
            lambda side: ebuf.at[pl.ds(aligned(row * size + side * half, 8), half), :],
            re,
            slots,
        )

    slots = [copies.slot() for _ in range(8)]
    own_left(near, slots, range(pairs))
    farther = [copies.slot() for _ in range(4)]

    r_ids = lax.broadcasted_iota(jnp.int32, (size, wide), 0)
    c_ids = lax.broadcasted_iota(jnp.int32, (size, wide), 1)
    place = jnp.where(c_ids == r_ids + odd * size, 1.0, 0.0).astype(jnp.float32)
    own[:, pl.ds(0, wide)] = dot(dinv[...], place)
    own[:, pl.ds(wide, rhs.shape[1])] = rhs[...]

    @pl.when(odd == 1)
    def _():
        pltpu.make_async_copy(dleft, dleft, rd).wait()
        left = dot(dinv[...], dot(corner[...], dleft[...]))
        lead = jnp.where(c_ids == r_ids, 1.0, 0.0).astype(jnp.float32)
        own[:, pl.ds(0, wide)] = own[:, pl.ds(0, wide)] - dot(left, lead)

    slots = [copies.slot() for _ in range(8)]
    own_right(near, slots)

    def view(kind, j, side):
        if kind == "left":
            return lbuf[j // 2].at[pl.ds(aligned((j % 2) * size + side * half, 8), half), :]
        return ebuf.at[pl.ds(aligned(j * size + side * half, 8), half), :]

    def sem_of(kind, j, side):
        return (rl if kind == "left" else re).at[j, side]

    def panels(kind, numbers):
        return [j for j in numbers if kind == "right" or j >= 2]

    def forward(kind, j, when, targets, beside_too):
        here, sem = view(kind, j, core), sem_of(kind, j, core)

        def pass_on():
            copies.arrived(here, sem)
            for to_x in targets:
                copies.remote(here, here, sem, at(to_x, z, core))
            if beside_too is not None:
                copies.group(
                    beside_too, lambda: copies.remote(here, here, sem, at(x, z, 1 - core))
                )

        copies.group(when, pass_on)

    def row_pass(kind, r, hops, targets, beside_too=True):
        for j in panels(kind, range(RING * r, RING * (r + 1))):
            apart = lax.rem(z + RING - j % RING, RING)
            when = lax.rem(apart, 2) == 1 if hops == 1 else apart == hops
            if r == RING - 1 and j % RING >= 2:
                when = when & (zhi == 1)
            forward(kind, j, when, targets, (mine >= j // 2) if beside_too else None)

    for r in range(RING):

        def own_row(r=r):
            relays = [(kind, q, RELAYED[q]) for q in RELAYED for kind in ("left", "right") if r == 0]

            def relay(kind, hops):
                for name, q, targets in relays:
                    if name == kind:
                        row_pass(kind, q, hops, targets, False)

            row_pass("left", r, 1, TARGETS[r])
            own_left(far, farther[:2], (2 * r, 2 * r + 1))
            relay("left", 0)
            row_pass("right", r, 1, TARGETS[r])
            own_right(far, farther[2:])
            relay("left", 1)
            row_pass("left", r, 2, TARGETS[r])
            row_pass("right", r, 2, TARGETS[r])
            relay("left", 2)
            for hops in range(3):
                relay("right", hops)

        copies.group(x == r, own_row)

    def take(m):
        def body():
            for kind in ("left", "right"):
                for j in panels(kind, (2 * m, 2 * m + 1)):
                    forward(kind, j, True, (), True)

        copies.group(x > m // 2, body)

    partner = at(x, z + 1 - 2 * odd, 1 - core)
    half_of_pair = jnp.where(home, odd, 1 - odd)
    edge = RING - 1
    row_lead = (zhi == 1) & (core == 0)
    last = row_lead & (x == edge)

    def solve(m):
        here = mine >= m

        def wait():
            for kind in ("left", "right"):
                for j in panels(kind, (2 * m, 2 * m + 1)):
                    pl.when(row == j)(
                        lambda kind=kind, j=j: copies.arrived(view(kind, j, core), sem_of(kind, j, core))
                    )
                    copies.arrived(view(kind, j, 1 - core), sem_of(kind, j, 1 - core))

        pl.when(here)(wait)
        block = xa.at[:, pl.ds(m * wide, wide)]

        @pl.when(mine == m)
        def _():
            block[...] = ebuf[pl.ds(aligned(m * wide + half_of_pair * size, 8), size), pl.ds(0, wide)]

        @pl.when(mine > m)
        def _():
            block[...] = dot3(split(block[...]), split(ebuf[pl.ds(m * wide, wide), pl.ds(0, wide)]))

        @pl.when(here)
        def _():
            solved = split(block[...])
            dloc[...] += dot3(
                solved, split(ebuf[pl.ds(m * wide, wide), pl.ds(wide, dloc.shape[1])])
            )
            parts[0, :, :], parts[1, :, :] = solved
            if m:

                @pl.loop(0, m)
                def _(n):
                    cols = pl.ds(pl.multiple_of(n * wide, wide), wide)
                    xa[:, cols] -= dot3((parts[0], parts[1]), split(lbuf[m][:, cols]))

        result = inv.at[:, pl.ds(m * wide, wide)]
        copies.group((mine < m) | home, lambda: copies.local(block, result, lx.at[m]))
        when = here & away
        if m < pairs // 2:
            when = when & jnp.logical_not(last)
        copies.group(when, lambda: copies.remote(block, result, rx.at[m], partner))

    for m in reversed(range(pairs)):
        solve(m)
        if 2 <= m:
            take(m - 2)
    width, columns = cpl.shape[0], dloc.shape[1]
    plane, which = lax.div(blk, 2), 1 - odd
    later = (plane > 0) | (which > 0)
    copies.arrived(cpl, rc)
    gain[...] = -dot(xa[:, pl.ds(0, width)], cpl[...])

    @pl.when(last | jnp.logical_not(later))
    def _():
        tail[...] = jnp.zeros_like(tail)

    @pl.when(last)
    def _():
        maps[which, :, pl.ds(0, width)] = gain[pl.ds(size - width, width), :]
        maps[which, :, pl.ds(width, columns)] = dloc[pl.ds(size - width, width), :]

    copies.group(last, lambda: copies.remote(maps.at[which], maps.at[which], rp, beside))

    def held_back():
        for m in reversed(range(pairs // 2)):
            cols = pl.ds(m * wide, wide)
            copies.remote(xa.at[:, cols], inv.at[:, cols], rx.at[m], partner)

    copies.group(last & away, held_back)

    @pl.when(last)
    def _():
        copies.arrived(maps.at[1 - which], rp)
        mine_map[...] = dot(maps[1, :, pl.ds(0, width)], maps[0, :, :])
        mine_map[:, pl.ds(width, columns)] += maps[1, :, pl.ds(width, columns)]

    for step, device in enumerate(others):
        copies.group(
            last & (plane + step + 1 < planes),
            lambda device=device: copies.remote(
                mine_map, joined.at[plane], rj.at[plane], device
            ),
        )

    def step_on(matrix_and_term):
        left = matrix_and_term[:, pl.ds(0, width)]
        tail[...] = dot(left, tail[...]) + matrix_and_term[:, pl.ds(width, columns)]

    for k in range(planes - 1):

        @pl.when(last & (plane > k))
        def _():
            copies.arrived(joined.at[k], rj.at[k])
            step_on(joined.at[k])

    @pl.when(last & (which == 1))
    def _():
        step_on(maps.at[0])

    def hand_out(devices):
        for device in devices:
            copies.remote(tail, tail, rt, device)

    pl.when(later & jnp.logical_not(last))(lambda: copies.arrived(tail, rt))
    copies.group(later & last, lambda: hand_out([at(to_x, z, 0) for to_x in range(edge)]))
    copies.group(
        later & row_lead, lambda: hand_out([at(x, z - 2, 0), at(x, z - 2, 1), at(x, z, 1)])
    )
    dloc[...] += dot(gain[...], tail[...])
    copies.group(home, lambda: copies.local(dloc, solved, lx.at[pairs]))
    copies.group(away, lambda: copies.remote(dloc, solved, rx.at[pairs], partner))

    @pl.when(away)
    def _():
        for m in range(pairs):
            result = inv.at[:, pl.ds(m * wide, wide)]
            pl.when(mine >= m)(lambda m=m, result=result: copies.arrived(result, rx.at[m]))
        copies.arrived(solved, rx.at[pairs])

    copies.finish()


def invert(factor, coupling, right_side):
    size, order = factor.shape
    columns, width = right_side.shape[1], coupling.shape[0]
    planes = lax.axis_size("blk") // 2
    pairs, wide = order // (2 * size), 2 * size
    row = lax.axis_index("row")
    diag = lax.dynamic_slice_in_dim(factor, row * size, size, 1)
    corner = lax.dynamic_slice_in_dim(factor, (row - row % 2) * size, size, 1)
    vmem = pl.BlockSpec(memory_space=pltpu.VMEM)
    hbm = pl.BlockSpec(memory_space=pl.ANY)
    dma = pltpu.SemaphoreType.DMA
    panels = 2 * pairs
    return pl.pallas_call(
        functools.partial(solve_kernel, pairs, planes),
        out_shape=(
            jax.ShapeDtypeStruct((size, order), jnp.float32),
            jax.ShapeDtypeStruct((size, columns), jnp.float32),
        ),
        in_specs=[vmem] * 5,
        out_specs=(hbm, hbm),
        scratch_shapes=[
            *[pltpu.VMEM((wide, wide * m), jnp.float32) for m in range(1, pairs)],
            pltpu.VMEM((order, wide + columns), jnp.float32),
            pltpu.VMEM((size, wide + columns), jnp.float32),
            pltpu.VMEM((size, order), jnp.float32),
            pltpu.VMEM((size, size), jnp.float32),
            pltpu.VMEM((size, size), jnp.float32),
            pltpu.VMEM((size, columns), jnp.float32),
            pltpu.VMEM((2, size, wide), jnp.bfloat16),
            pltpu.VMEM((width, width), jnp.float32),
            pltpu.VMEM((size, width), jnp.float32),
            pltpu.VMEM((2, width, width + columns), jnp.float32),
            pltpu.VMEM((width, width + columns), jnp.float32),
            pltpu.VMEM((planes, width, width + columns), jnp.float32),
            pltpu.VMEM((width, columns), jnp.float32),
            dma((400,)),
            dma((panels, 2)),
            dma((panels, 2)),
            dma((pairs + 1,)),
            dma,
            dma((pairs + 1,)),
            dma,
            dma,
            dma((planes,)),
            dma,
        ],
        compiler_params=pltpu.CompilerParams(
            collective_id=0, has_side_effects=True, vmem_limit_bytes=52 * 1024 * 1024
        ),
    )(factor, diag, corner, right_side, coupling)


def on_device(factor, coupling, right_side):
    inverse, solved = invert(factor[0], coupling[0], right_side[0])
    return inverse[None], solved[None]


def solution(mesh):
    in_specs = (P("blk", "row", None), P("blk", None, None), P("blk", "row", None))
    out_specs = (P("blk", "row", None), P("blk", "row", None))
    return jax.shard_map(
        on_device, mesh=mesh, in_specs=in_specs, out_specs=out_specs, check_vma=False
    )
```

```python
import functools

import jax
import jax.numpy as jnp
from jax import lax
from jax.experimental import pallas as pl
from jax.experimental.pallas import tpu as pltpu
from jax.sharding import PartitionSpec as P

MESH = pl.DeviceIdType.MESH
RING = 4
TARGETS = {0: (3, 1, 2), 1: (0, 2), 2: (3,), 3: ()}
TURNED = (2,)
RELAYED = {1: (3,)}


def dot(a, b):
    return jnp.dot(a, b, precision=lax.Precision.HIGHEST, preferred_element_type=jnp.float32)


def split(a):
    high = a.astype(jnp.bfloat16)
    return high, (a - high.astype(jnp.float32)).astype(jnp.bfloat16)


def dot3(a, b):
    (a_high, a_low), (b_high, b_low) = a, b

    def one(p, q):
        return jnp.dot(p, q, preferred_element_type=jnp.float32)

    return one(a_high, b_high) + (one(a_high, b_low) + one(a_low, b_high))


def unit_lower_inverse(matrix):
    size = matrix.shape[0]
    rows = lax.broadcasted_iota(jnp.int32, (size, size), 0)
    cols = lax.broadcasted_iota(jnp.int32, (size, size), 1)
    inverse = jnp.where(rows == cols, 1.0, 0.0).astype(jnp.float32)
    bit = 0
    while (1 << bit) < size:
        same = (rows >> (bit + 1)) == (cols >> (bit + 1))
        corner = same & (((rows >> bit) & 1) == 1) & (((cols >> bit) & 1) == 0)
        below = jnp.where(corner, matrix, 0.0)
        if bit == 0:
            inverse = inverse - below
        else:
            inverse = inverse - dot(dot(inverse, below), inverse)
        bit += 1
    return inverse


class Copies:
    def __init__(self, sems):
        self.sems, self.used, self.groups, self.depth, self.ending = sems, 0, [], 0, False

    def slot(self):
        self.used += 1
        return self.used - 1

    def group(self, when, body):
        if not self.depth and not self.ending:
            self.groups.append((when, body, self.used))
        self.depth += 1
        pl.when(when)(lambda: body())
        self.depth -= 1

    def arrived(self, target, sem):
        if not self.ending:
            pltpu.make_async_copy(target, target, sem).wait()

    def remote(self, source, target, arrival, device, slot=None):
        copy = pltpu.make_async_remote_copy(
            src_ref=source,
            dst_ref=target,
            send_sem=self.sems.at[self.slot() if slot is None else slot],
            recv_sem=arrival,
            device_id=device,
            device_id_type=MESH,
        )
        if self.ending:
            copy.wait_send()
        else:
            copy.start()

    def local(self, source, target, sem, waited=True):
        copy = pltpu.make_async_copy(source, target, sem)
        if not self.ending:
            copy.start()
        elif waited:
            copy.wait()

    def finish(self):
        self.ending = True
        for when, body, self.used in self.groups:
            self.group(when, body)


def solve_kernel(pairs, planes, fac, rhs, coupling, inv, solved, *scratch):
    lbuf = (None, *scratch[: pairs - 1])
    ebuf, own, xa, dinv, dleft, dloc, parts, cpl, gain, maps, mine_map, joined, tail = scratch[
        pairs - 1 : pairs + 12
    ]
    sends, rl, re, rx, rd, lx, rc, rp, rj, rt = scratch[pairs + 12 :]
    size = fac.shape[0]
    half, wide = size // 2, 2 * size
    lead, unit = rhs.shape[1], min(128, size)
    widths = (lead + -(-size // unit) * unit, lead + wide)
    blk, row = lax.axis_index("blk"), lax.axis_index("row")
    core = lax.rem(blk, 2)
    x, z = lax.div(row, RING), lax.rem(row, RING)
    zhi, odd = lax.div(z, 2), lax.rem(z, 2)
    mine = 2 * x + zhi
    home = core == 1 - odd
    away = core == odd
    first = blk - core

    def at(to_x, to_z, to_core):
        return {"blk": first + to_core, "row": to_x * RING + to_z}

    def aligned(index, by):
        return pl.multiple_of(index, by)

    barrier = pltpu.get_barrier_semaphore()
    peers = [(x, z, 1 - core)]
    for step in range(1, RING):
        for side in range(2):
            peers += [(x, lax.rem(z + step, RING), side), (lax.rem(x + step, RING), z, side)]
    others = [
        {"blk": lax.rem(blk + 2 * step, 2 * planes), "row": row} for step in range(1, planes)
    ]
    peers = [at(*peer) for peer in peers] + others
    for peer in peers:
        pl.semaphore_signal(barrier, inc=1, device_id=peer, device_id_type=MESH)

    edge = RING - 1
    row_lead = (zhi == 1) & (core == 0)
    last = row_lead & (x == edge)
    led = (zhi == 0) & (core == 0) & (x != edge)
    over = [at(to_x, lax.rem(z + 2, RING), 0) for to_x in range(edge)]

    @pl.when(last)
    def _():
        for peer in over:
            pl.semaphore_signal(barrier, inc=1, device_id=peer, device_id_type=MESH)

    @pl.when(led)
    def _():
        lead_of = at(edge, lax.rem(z + 2, RING), 0)
        pl.semaphore_signal(barrier, inc=1, device_id=lead_of, device_id_type=MESH)

    xa[...] = jnp.zeros_like(xa)
    dloc[...] = jnp.zeros_like(dloc)
    for m in range(pairs):
        rest = pl.ds(widths[0], widths[1] - widths[0])
        ebuf[pl.ds(m * wide, size), rest] = jnp.zeros((size, widths[1] - widths[0]), jnp.float32)
    frame = fac[:, pl.ds(aligned(mine * wide, wide), wide)]
    turned = pltpu.roll(frame, size, 1)
    dinv[...] = unit_lower_inverse(jnp.where(odd == 1, turned, frame)[:, :size])
    extra = jnp.where(last, len(over), jnp.where(led, 1, 0))
    pl.semaphore_wait(barrier, len(peers) + extra)

    copies = Copies(sends)
    beside = at(x, z + 1 - 2 * odd, core)

    def share_coupling():
        copies.local(coupling, cpl, rc, waited=False)
        copies.remote(coupling, cpl, rc, at(x, z, 1 - core))

    copies.group(home, share_coupling)
    copies.group(odd == 0, lambda: copies.remote(dinv, dleft, rd, beside))

    def near(source, target, arrival, slots):
        sides = [(source(side), target(side), arrival.at[row, side], side) for side in range(2)]

        def at_home():
            for src, dst, sem, side in sides:
                copies.remote(src, dst, sem, at(x, z, 1 - core), slots[side])
                copies.local(src, dst, sem, waited=False)

        def along(targets):
            for number, to_x in enumerate(targets):
                for src, dst, sem, side in sides:
                    copies.remote(src, dst, sem, at(to_x, z, side), slots[2 * number + 2 + side])

        copies.group(home, at_home)
        for r, targets in TARGETS.items():
            if targets:
                copies.group(home & (x == r), functools.partial(along, targets))
        for number, step in enumerate((1, 3)):
            to_z = lax.rem(z + step, RING)

            def beside(number=number, to_z=to_z):
                for src, dst, sem, side in sides:
                    copies.remote(src, dst, sem, at(x, to_z, side), slots[2 * number + side])

            copies.group(away & wanted(to_z), beside)

    def far(source, target, arrival, slots):
        to_z = lax.rem(z + 2, RING)

        def across():
            for side in range(2):
                copies.remote(
                    source(side), target(side), arrival.at[row, side], at(x, to_z, side), slots[side]
                )

        copies.group(home & wanted(to_z), across)

    def wanted(to_z):
        return (x < RING - 1) | (zhi == 0) | (lax.div(to_z, 2) == 1)

    def own_left(how, slots, numbers):
        for m in numbers:
            if m == 0:
                continue
            copies.group(
                mine == m,
                lambda m=m: how(
                    lambda side: fac.at[pl.ds(side * half, half), pl.ds(0, wide * m)],
                    lambda side: lbuf[m].at[pl.ds(aligned(odd * size + side * half, 8), half), :],
                    rl,
                    slots,
                ),
            )

    def own_right(how, slots):
        for parity, width in enumerate(widths):
            cols = pl.ds(0, width)
            copies.group(
                odd == parity,
                lambda cols=cols: how(
                    lambda side: own.at[pl.ds(side * half, half), cols],
                    lambda side: ebuf.at[pl.ds(aligned(row * size + side * half, 8), half), cols],
                    re,
                    slots,
                ),
            )

    slots = [copies.slot() for _ in range(8)]
    own_left(near, slots, range(pairs))
    farther = [copies.slot() for _ in range(4)]

    r_ids = lax.broadcasted_iota(jnp.int32, (size, wide), 0)
    c_ids = lax.broadcasted_iota(jnp.int32, (size, wide), 1)
    place = jnp.where(c_ids == r_ids + odd * size, 1.0, 0.0).astype(jnp.float32)
    own[:, pl.ds(lead, wide)] = dot(dinv[...], place)
    own[:, pl.ds(0, lead)] = rhs[...]

    @pl.when(odd == 1)
    def _():
        pltpu.make_async_copy(dleft, dleft, rd).wait()
        left = dot(dinv[...], dot(fac[:, pl.ds(aligned(mine * wide, wide), wide)][:, :size], dleft[...]))
        front = jnp.where(c_ids == r_ids, 1.0, 0.0).astype(jnp.float32)
        own[:, pl.ds(lead, wide)] = own[:, pl.ds(lead, wide)] - dot(left, front)

    slots = [copies.slot() for _ in range(8)]
    own_right(near, slots)

    def view(kind, j, side):
        if kind == "left":
            return lbuf[j // 2].at[pl.ds(aligned((j % 2) * size + side * half, 8), half), :]
        cols = pl.ds(0, widths[j % 2])
        return ebuf.at[pl.ds(aligned(j * size + side * half, 8), half), cols]

    def sem_of(kind, j, side):
        return (rl if kind == "left" else re).at[j, side]

    def panels(kind, numbers):
        return [j for j in numbers if kind == "right" or j >= 2]

    def forward(kind, j, when, targets, beside_too, across=False):
        here, sem = view(kind, j, core), sem_of(kind, j, core)

        def pass_on():
            copies.arrived(here, sem)
            for to_x in targets:
                copies.remote(here, here, sem, at(to_x, z, core))
            if across:
                copies.remote(here, here, sem, at(x, lax.rem(z + 2, RING), core))
            if beside_too is not None:
                copies.group(
                    beside_too, lambda: copies.remote(here, here, sem, at(x, z, 1 - core))
                )

        copies.group(when, pass_on)

    def row_pass(kind, r, hops, targets, beside_too=True):
        for j in panels(kind, range(RING * r, RING * (r + 1))):
            apart = lax.rem(z + RING - j % RING, RING)
            when = lax.rem(apart, 2) == 1 if hops == 1 else apart == hops
            if r == RING - 1 and j % RING >= 2:
                when = when & (zhi == 1)
            forward(kind, j, when, targets, (mine >= j // 2) if beside_too else None)

    def turn(kind, r):
        for q in TURNED:
            if q + 1 == r:
                for j in panels(kind, range(RING * q, RING * (q + 1))):
                    forward(kind, j, z == j % RING, (), mine >= j // 2, across=True)

    for r in range(RING):

        def own_row(r=r):
            relays = [(kind, q, RELAYED[q]) for q in RELAYED for kind in ("left", "right") if r == 0]

            def relay(kind, hops):
                for name, q, targets in relays:
                    if name == kind:
                        row_pass(kind, q, hops, targets, False)

            row_pass("left", r, 1, TARGETS[r])
            own_left(far, farther[:2], (2 * r, 2 * r + 1))
            turn("left", r)
            relay("left", 0)
            row_pass("right", r, 1, TARGETS[r])
            own_right(far, farther[2:])
            turn("right", r)
            relay("left", 1)
            onward = () if r in TURNED else TARGETS[r]
            row_pass("left", r, 2, onward)
            row_pass("right", r, 2, onward)
            relay("left", 2)
            for hops in range(3):
                relay("right", hops)

        copies.group(x == r, own_row)

    def take(m):
        def body():
            for kind in ("left", "right"):
                for j in panels(kind, (2 * m, 2 * m + 1)):
                    when = (z != j % RING) if m // 2 in TURNED else True
                    forward(kind, j, when, (), True)

        copies.group(x > m // 2, body)

    partner = at(x, z + 1 - 2 * odd, 1 - core)
    half_of_pair = jnp.where(home, odd, 1 - odd)

    def solve(m):
        here = mine >= m

        def wait():
            for kind in ("left", "right"):
                for j in panels(kind, (2 * m, 2 * m + 1)):
                    pl.when(row == j)(
                        lambda kind=kind, j=j: copies.arrived(view(kind, j, core), sem_of(kind, j, core))
                    )
                    copies.arrived(view(kind, j, 1 - core), sem_of(kind, j, 1 - core))

        pl.when(here)(wait)
        block = xa.at[:, pl.ds(m * wide, wide)]

        @pl.when(mine == m)
        def _():
            rows = pl.ds(aligned(m * wide + half_of_pair * size, 8), size)
            block[...] = ebuf[rows, pl.ds(lead, wide)]

        @pl.when(mine > m)
        def _():
            block[...] = dot3(split(block[...]), split(ebuf[pl.ds(m * wide, wide), pl.ds(lead, wide)]))

        @pl.when(here)
        def _():
            solved = split(block[...])
            dloc[...] += dot3(
                solved, split(ebuf[pl.ds(m * wide, wide), pl.ds(0, lead)])
            )
            parts[0, :, :], parts[1, :, :] = solved
            if m:

                @pl.loop(0, m)
                def _(n):
                    cols = pl.ds(pl.multiple_of(n * wide, wide), wide)
                    xa[:, cols] -= dot3((parts[0], parts[1]), split(lbuf[m][:, cols]))

        result = inv.at[:, pl.ds(m * wide, wide)]
        copies.group((mine < m) | home, lambda: copies.local(block, result, lx.at[m]))
        when = here & away
        if m < pairs // 2:
            when = when & jnp.logical_not(last)
        copies.group(when, lambda: copies.remote(block, result, rx.at[m], partner))

    for m in reversed(range(pairs)):
        solve(m)
        if 2 <= m:
            take(m - 2)
    width, columns = cpl.shape[0], dloc.shape[1]
    plane, which = lax.div(blk, 2), 1 - odd
    later = (plane > 0) | (which > 0)
    copies.arrived(cpl, rc)
    gain[...] = -dot(xa[:, pl.ds(0, width)], cpl[...])

    @pl.when(last | jnp.logical_not(later))
    def _():
        tail[...] = jnp.zeros_like(tail)

    @pl.when(last)
    def _():
        maps[which, :, pl.ds(0, width)] = gain[pl.ds(size - width, width), :]
        maps[which, :, pl.ds(width, columns)] = dloc[pl.ds(size - width, width), :]

    copies.group(last, lambda: copies.remote(maps.at[which], maps.at[which], rp, beside))

    def held_back():
        for m in reversed(range(pairs // 2)):
            cols = pl.ds(m * wide, wide)
            copies.remote(xa.at[:, cols], inv.at[:, cols], rx.at[m], partner)

    copies.group(last & away, held_back)

    @pl.when(last)
    def _():
        copies.arrived(maps.at[1 - which], rp)
        mine_map[...] = dot(maps[1, :, pl.ds(0, width)], maps[0, :, :])
        mine_map[:, pl.ds(width, columns)] += maps[1, :, pl.ds(width, columns)]

    for step, device in enumerate(others):
        copies.group(
            last & (plane + step + 1 < planes),
            lambda device=device: copies.remote(
                mine_map, joined.at[plane], rj.at[plane], device
            ),
        )

    def step_on(matrix_and_term):
        left = matrix_and_term[:, pl.ds(0, width)]
        tail[...] = dot(left, tail[...]) + matrix_and_term[:, pl.ds(width, columns)]

    for k in range(planes - 1):

        @pl.when(last & (plane > k))
        def _():
            copies.arrived(joined.at[k], rj.at[k])
            step_on(joined.at[k])

    @pl.when(last & (which == 1))
    def _():
        step_on(maps.at[0])

    def hand_out(devices):
        for device in devices:
            copies.remote(tail, tail, rt, device)

    pl.when(later & jnp.logical_not(last))(lambda: copies.arrived(tail, rt))
    ahead = [at(to_x, z, 0) for to_x in range(edge)]
    copies.group(later & last, lambda: hand_out([over[0], *ahead, *over[1:], at(x, z, 1)]))
    copies.group(
        later & led & (x == 0), lambda: hand_out([at(edge, z, 0), at(edge, z, 1)])
    )
    copies.group(
        later & (core == 0) & (x != edge), lambda: hand_out([at(x, z, 1)])
    )
    dloc[...] += dot(gain[...], tail[...])
    copies.group(home, lambda: copies.local(dloc, solved, lx.at[pairs]))
    copies.group(away, lambda: copies.remote(dloc, solved, rx.at[pairs], partner))

    @pl.when(away)
    def _():
        for m in range(pairs):
            result = inv.at[:, pl.ds(m * wide, wide)]
            pl.when(mine >= m)(lambda m=m, result=result: copies.arrived(result, rx.at[m]))
        copies.arrived(solved, rx.at[pairs])

    copies.finish()


def invert(factor, coupling, right_side):
    size, order = factor.shape
    columns, width = right_side.shape[1], coupling.shape[0]
    planes = lax.axis_size("blk") // 2
    pairs, wide = order // (2 * size), 2 * size
    vmem = pl.BlockSpec(memory_space=pltpu.VMEM)
    hbm = pl.BlockSpec(memory_space=pl.ANY)
    dma = pltpu.SemaphoreType.DMA
    panels = 2 * pairs
    return pl.pallas_call(
        functools.partial(solve_kernel, pairs, planes),
        out_shape=(
            jax.ShapeDtypeStruct((size, order), jnp.float32),
            jax.ShapeDtypeStruct((size, columns), jnp.float32),
        ),
        in_specs=[vmem] * 3,
        out_specs=(hbm, hbm),
        scratch_shapes=[
            *[pltpu.VMEM((wide, wide * m), jnp.float32) for m in range(1, pairs)],
            pltpu.VMEM((order, wide + columns), jnp.float32),
            pltpu.VMEM((size, wide + columns), jnp.float32),
            pltpu.VMEM((size, order), jnp.float32),
            pltpu.VMEM((size, size), jnp.float32),
            pltpu.VMEM((size, size), jnp.float32),
            pltpu.VMEM((size, columns), jnp.float32),
            pltpu.VMEM((2, size, wide), jnp.bfloat16),
            pltpu.VMEM((width, width), jnp.float32),
            pltpu.VMEM((size, width), jnp.float32),
            pltpu.VMEM((2, width, width + columns), jnp.float32),
            pltpu.VMEM((width, width + columns), jnp.float32),
            pltpu.VMEM((planes, width, width + columns), jnp.float32),
            pltpu.VMEM((width, columns), jnp.float32),
            dma((400,)),
            dma((panels, 2)),
            dma((panels, 2)),
            dma((pairs + 1,)),
            dma,
            dma((pairs + 1,)),
            dma,
            dma,
            dma((planes,)),
            dma,
        ],
        compiler_params=pltpu.CompilerParams(
            collective_id=0, has_side_effects=True, vmem_limit_bytes=52 * 1024 * 1024
        ),
    )(factor, right_side, coupling)


def on_device(factor, coupling, right_side):
    inverse, solved = invert(factor[0], coupling[0], right_side[0])
    return inverse[None], solved[None]


def solution(mesh):
    in_specs = (P("blk", "row", None), P("blk", None, None), P("blk", "row", None))
    out_specs = (P("blk", "row", None), P("blk", "row", None))
    return jax.shard_map(
        on_device, mesh=mesh, in_specs=in_specs, out_specs=out_specs, check_vma=False
    )
```

```python
import functools

import jax
import jax.numpy as jnp
from jax import lax
from jax.experimental import pallas as pl
from jax.experimental.pallas import tpu as pltpu
from jax.sharding import PartitionSpec as P

MESH = pl.DeviceIdType.MESH
RING = 4
TARGETS = {0: (3, 1, 2), 1: (0, 2), 2: (3,), 3: ()}
TURNED = (2,)
RELAYED = {1: (3,)}


def dot(a, b):
    return jnp.dot(a, b, precision=lax.Precision.HIGHEST, preferred_element_type=jnp.float32)


def split(a):
    high = a.astype(jnp.bfloat16)
    return high, (a - high.astype(jnp.float32)).astype(jnp.bfloat16)


def dot3(a, b):
    (a_high, a_low), (b_high, b_low) = a, b

    def one(p, q):
        return jnp.dot(p, q, preferred_element_type=jnp.float32)

    return one(a_high, b_high) + (one(a_high, b_low) + one(a_low, b_high))


def unit_lower_inverse(matrix):
    size = matrix.shape[0]
    rows = lax.broadcasted_iota(jnp.int32, (size, size), 0)
    cols = lax.broadcasted_iota(jnp.int32, (size, size), 1)
    inverse = jnp.where(rows == cols, 1.0, 0.0).astype(jnp.float32)
    bit = 0
    while (1 << bit) < size:
        same = (rows >> (bit + 1)) == (cols >> (bit + 1))
        corner = same & (((rows >> bit) & 1) == 1) & (((cols >> bit) & 1) == 0)
        below = jnp.where(corner, matrix, 0.0)
        if bit == 0:
            inverse = inverse - below
        else:
            inverse = inverse - dot(dot(inverse, below), inverse)
        bit += 1
    return inverse


class Copies:
    def __init__(self, sems):
        self.sems, self.used, self.groups, self.depth, self.ending = sems, 0, [], 0, False

    def slot(self):
        self.used += 1
        return self.used - 1

    def group(self, when, body):
        if not self.depth and not self.ending:
            self.groups.append((when, body, self.used))
        self.depth += 1
        pl.when(when)(lambda: body())
        self.depth -= 1

    def arrived(self, target, sem):
        if not self.ending:
            pltpu.make_async_copy(target, target, sem).wait()

    def remote(self, source, target, arrival, device, slot=None):
        copy = pltpu.make_async_remote_copy(
            src_ref=source,
            dst_ref=target,
            send_sem=self.sems.at[self.slot() if slot is None else slot],
            recv_sem=arrival,
            device_id=device,
            device_id_type=MESH,
        )
        if self.ending:
            copy.wait_send()
        else:
            copy.start()

    def local(self, source, target, sem, waited=True):
        copy = pltpu.make_async_copy(source, target, sem)
        if not self.ending:
            copy.start()
        elif waited:
            copy.wait()

    def finish(self):
        self.ending = True
        for when, body, self.used in self.groups:
            self.group(when, body)


def solve_kernel(pairs, planes, fac, rhs, coupling, inv, solved, *scratch):
    lbuf = (None, *scratch[: pairs - 1])
    ebuf, own, xa, dinv, dleft, dloc, parts, cpl, gain, maps, mine_map, joined, tail, frames = scratch[
        pairs - 1 : pairs + 13
    ]
    sends, rl, re, rx, rd, lx, rc, rp, rj, rt, lf = scratch[pairs + 13 :]
    size = fac.shape[0]
    half, wide = size // 2, 2 * size
    lead, unit = rhs.shape[1], min(128, size)
    widths = (lead + -(-size // unit) * unit, lead + wide)
    blk, row = lax.axis_index("blk"), lax.axis_index("row")
    core = lax.rem(blk, 2)
    x, z = lax.div(row, RING), lax.rem(row, RING)
    zhi, odd = lax.div(z, 2), lax.rem(z, 2)
    mine = 2 * x + zhi
    home = core == 1 - odd
    away = core == odd
    first = blk - core

    def at(to_x, to_z, to_core):
        return {"blk": first + to_core, "row": to_x * RING + to_z}

    def aligned(index, by):
        return pl.multiple_of(index, by)

    barrier = pltpu.get_barrier_semaphore()
    peers = [(x, z, 1 - core)]
    for step in range(1, RING):
        for side in range(2):
            peers += [(x, lax.rem(z + step, RING), side), (lax.rem(x + step, RING), z, side)]
    others = [
        {"blk": lax.rem(blk + 2 * step, 2 * planes), "row": row} for step in range(1, planes)
    ]
    peers = [at(*peer) for peer in peers] + others
    for peer in peers:
        pl.semaphore_signal(barrier, inc=1, device_id=peer, device_id_type=MESH)

    edge = RING - 1
    row_lead = (zhi == 1) & (core == 0)
    last = row_lead & (x == edge)
    led = (zhi == 0) & (core == 0) & (x != edge)
    over = [at(to_x, lax.rem(z + 2, RING), 0) for to_x in range(edge)]

    @pl.when(last)
    def _():
        for peer in over:
            pl.semaphore_signal(barrier, inc=1, device_id=peer, device_id_type=MESH)

    @pl.when(led)
    def _():
        lead_of = at(edge, lax.rem(z + 2, RING), 0)
        pl.semaphore_signal(barrier, inc=1, device_id=lead_of, device_id_type=MESH)

    xa[...] = jnp.zeros_like(xa)
    dloc[...] = jnp.zeros_like(dloc)
    for m in range(pairs):
        rest = pl.ds(widths[0], widths[1] - widths[0])
        ebuf[pl.ds(m * wide, size), rest] = jnp.zeros((size, widths[1] - widths[0]), jnp.float32)
    part_of = pltpu.make_async_copy(fac.at[:, pl.ds(aligned(mine * wide, wide), wide)], frames, lf)
    part_of.start()
    part_of.wait()
    frame = frames[...]
    turned = pltpu.roll(frame, size, 1)
    dinv[...] = unit_lower_inverse(jnp.where(odd == 1, turned, frame)[:, :size])
    extra = jnp.where(last, len(over), jnp.where(led, 1, 0))
    pl.semaphore_wait(barrier, len(peers) + extra)

    copies = Copies(sends)
    beside = at(x, z + 1 - 2 * odd, core)

    def share_coupling():
        copies.local(coupling, cpl, rc, waited=False)
        copies.remote(coupling, cpl, rc, at(x, z, 1 - core))

    copies.group(home, share_coupling)
    copies.group(odd == 0, lambda: copies.remote(dinv, dleft, rd, beside))

    def near(source, target, arrival, slots):
        sides = [(source(side), target(side), arrival.at[row, side], side) for side in range(2)]

        def at_home():
            for src, dst, sem, side in sides:
                copies.remote(src, dst, sem, at(x, z, 1 - core), slots[side])
                copies.local(src, dst, sem, waited=False)

        def along(targets):
            for number, to_x in enumerate(targets):
                for src, dst, sem, side in sides:
                    copies.remote(src, dst, sem, at(to_x, z, side), slots[2 * number + 2 + side])

        copies.group(home, at_home)
        for r, targets in TARGETS.items():
            if targets:
                copies.group(home & (x == r), functools.partial(along, targets))
        for number, step in enumerate((1, 3)):
            to_z = lax.rem(z + step, RING)

            def beside(number=number, to_z=to_z):
                for src, dst, sem, side in sides:
                    copies.remote(src, dst, sem, at(x, to_z, side), slots[2 * number + side])

            copies.group(away & wanted(to_z), beside)

    def far(source, target, arrival, slots):
        to_z = lax.rem(z + 2, RING)

        def across():
            for side in range(2):
                copies.remote(
                    source(side), target(side), arrival.at[row, side], at(x, to_z, side), slots[side]
                )

        copies.group(home & wanted(to_z), across)

    def wanted(to_z):
        return (x < RING - 1) | (zhi == 0) | (lax.div(to_z, 2) == 1)

    def own_left(how, slots, numbers):
        for m in numbers:
            if m == 0:
                continue
            copies.group(
                mine == m,
                lambda m=m: how(
                    lambda side: fac.at[pl.ds(side * half, half), pl.ds(0, wide * m)],
                    lambda side: lbuf[m].at[pl.ds(aligned(odd * size + side * half, 8), half), :],
                    rl,
                    slots,
                ),
            )

    def own_right(how, slots):
        for parity, width in enumerate(widths):
            cols = pl.ds(0, width)
            copies.group(
                odd == parity,
                lambda cols=cols: how(
                    lambda side: own.at[pl.ds(side * half, half), cols],
                    lambda side: ebuf.at[pl.ds(aligned(row * size + side * half, 8), half), cols],
                    re,
                    slots,
                ),
            )

    slots = [copies.slot() for _ in range(8)]
    own_left(near, slots, range(pairs))
    farther = [copies.slot() for _ in range(4)]

    r_ids = lax.broadcasted_iota(jnp.int32, (size, wide), 0)
    c_ids = lax.broadcasted_iota(jnp.int32, (size, wide), 1)
    place = jnp.where(c_ids == r_ids + odd * size, 1.0, 0.0).astype(jnp.float32)
    own[:, pl.ds(lead, wide)] = dot(dinv[...], place)
    own[:, pl.ds(0, lead)] = rhs[...]

    @pl.when(odd == 1)
    def _():
        pltpu.make_async_copy(dleft, dleft, rd).wait()
        left = dot(dinv[...], dot(frames[:, :size], dleft[...]))
        front = jnp.where(c_ids == r_ids, 1.0, 0.0).astype(jnp.float32)
        own[:, pl.ds(lead, wide)] = own[:, pl.ds(lead, wide)] - dot(left, front)

    slots = [copies.slot() for _ in range(8)]
    own_right(near, slots)

    def view(kind, j, side):
        if kind == "left":
            return lbuf[j // 2].at[pl.ds(aligned((j % 2) * size + side * half, 8), half), :]
        cols = pl.ds(0, widths[j % 2])
        return ebuf.at[pl.ds(aligned(j * size + side * half, 8), half), cols]

    def sem_of(kind, j, side):
        return (rl if kind == "left" else re).at[j, side]

    def panels(kind, numbers):
        return [j for j in numbers if kind == "right" or j >= 2]

    def forward(kind, j, when, targets, beside_too, across=False):
        here, sem = view(kind, j, core), sem_of(kind, j, core)

        def pass_on():
            copies.arrived(here, sem)
            for to_x in targets:
                copies.remote(here, here, sem, at(to_x, z, core))
            if across:
                copies.remote(here, here, sem, at(x, lax.rem(z + 2, RING), core))
            if beside_too is not None:
                copies.group(
                    beside_too, lambda: copies.remote(here, here, sem, at(x, z, 1 - core))
                )

        copies.group(when, pass_on)

    def row_pass(kind, r, hops, targets, beside_too=True):
        for j in panels(kind, range(RING * r, RING * (r + 1))):
            apart = lax.rem(z + RING - j % RING, RING)
            when = lax.rem(apart, 2) == 1 if hops == 1 else apart == hops
            if r == RING - 1 and j % RING >= 2:
                when = when & (zhi == 1)
            forward(kind, j, when, targets, (mine >= j // 2) if beside_too else None)

    def turn(kind, r):
        for q in TURNED:
            if q + 1 == r:
                for j in panels(kind, range(RING * q, RING * (q + 1))):
                    forward(kind, j, z == j % RING, (), mine >= j // 2, across=True)

    for r in range(RING):

        def own_row(r=r):
            relays = [(kind, q, RELAYED[q]) for q in RELAYED for kind in ("left", "right") if r == 0]

            def relay(kind, hops):
                for name, q, targets in relays:
                    if name == kind:
                        row_pass(kind, q, hops, targets, False)

            row_pass("left", r, 1, TARGETS[r])
            own_left(far, farther[:2], (2 * r, 2 * r + 1))
            turn("left", r)
            relay("left", 0)
            row_pass("right", r, 1, TARGETS[r])
            own_right(far, farther[2:])
            turn("right", r)
            relay("left", 1)
            onward = () if r in TURNED else TARGETS[r]
            row_pass("left", r, 2, onward)
            row_pass("right", r, 2, onward)
            relay("left", 2)
            for hops in range(3):
                relay("right", hops)

        copies.group(x == r, own_row)

    def take(m):
        def body():
            for kind in ("left", "right"):
                for j in panels(kind, (2 * m, 2 * m + 1)):
                    when = (z != j % RING) if m // 2 in TURNED else True
                    forward(kind, j, when, (), True)

        copies.group(x > m // 2, body)

    partner = at(x, z + 1 - 2 * odd, 1 - core)
    half_of_pair = jnp.where(home, odd, 1 - odd)

    def solve(m):
        here = mine >= m

        def wait():
            for kind in ("left", "right"):
                for j in panels(kind, (2 * m, 2 * m + 1)):
                    pl.when(row == j)(
                        lambda kind=kind, j=j: copies.arrived(view(kind, j, core), sem_of(kind, j, core))
                    )
                    copies.arrived(view(kind, j, 1 - core), sem_of(kind, j, 1 - core))

        pl.when(here)(wait)
        block = xa.at[:, pl.ds(m * wide, wide)]

        @pl.when(mine == m)
        def _():
            rows = pl.ds(aligned(m * wide + half_of_pair * size, 8), size)
            block[...] = ebuf[rows, pl.ds(lead, wide)]

        @pl.when(mine > m)
        def _():
            block[...] = dot3(split(block[...]), split(ebuf[pl.ds(m * wide, wide), pl.ds(lead, wide)]))

        @pl.when(here)
        def _():
            solved = split(block[...])
            dloc[...] += dot3(
                solved, split(ebuf[pl.ds(m * wide, wide), pl.ds(0, lead)])
            )
            parts[0, :, :], parts[1, :, :] = solved
            if m:

                @pl.loop(0, m)
                def _(n):
                    cols = pl.ds(pl.multiple_of(n * wide, wide), wide)
                    xa[:, cols] -= dot3((parts[0], parts[1]), split(lbuf[m][:, cols]))

        result = inv.at[:, pl.ds(m * wide, wide)]
        copies.group((mine < m) | home, lambda: copies.local(block, result, lx.at[m]))
        when = here & away
        if m < pairs // 2:
            when = when & jnp.logical_not(last)
        copies.group(when, lambda: copies.remote(block, result, rx.at[m], partner))

    for m in reversed(range(pairs)):
        solve(m)
        if 2 <= m:
            take(m - 2)
    width, columns = cpl.shape[0], dloc.shape[1]
    plane, which = lax.div(blk, 2), 1 - odd
    later = (plane > 0) | (which > 0)
    copies.arrived(cpl, rc)
    gain[...] = -dot3(split(xa[:, pl.ds(0, width)]), split(cpl[...]))

    @pl.when(last | jnp.logical_not(later))
    def _():
        tail[...] = jnp.zeros_like(tail)

    @pl.when(last)
    def _():
        maps[which, :, pl.ds(0, width)] = gain[pl.ds(size - width, width), :]
        maps[which, :, pl.ds(width, columns)] = dloc[pl.ds(size - width, width), :]

    copies.group(last, lambda: copies.remote(maps.at[which], maps.at[which], rp, beside))

    def held_back():
        for m in reversed(range(pairs // 2)):
            cols = pl.ds(m * wide, wide)
            copies.remote(xa.at[:, cols], inv.at[:, cols], rx.at[m], partner)

    copies.group(last & away, held_back)

    @pl.when(last)
    def _():
        copies.arrived(maps.at[1 - which], rp)
        mine_map[...] = dot3(split(maps[1, :, pl.ds(0, width)]), split(maps[0, :, :]))
        mine_map[:, pl.ds(width, columns)] += maps[1, :, pl.ds(width, columns)]

    for step, device in enumerate(others):
        copies.group(
            last & (plane + step + 1 < planes),
            lambda device=device: copies.remote(
                mine_map, joined.at[plane], rj.at[plane], device
            ),
        )

    def step_on(matrix_and_term):
        left = matrix_and_term[:, pl.ds(0, width)]
        tail[...] = dot3(split(left), split(tail[...])) + matrix_and_term[:, pl.ds(width, columns)]

    for k in range(planes - 1):

        @pl.when(last & (plane > k))
        def _():
            copies.arrived(joined.at[k], rj.at[k])
            step_on(joined.at[k])

    @pl.when(last & (which == 1))
    def _():
        step_on(maps.at[0])

    def hand_out(devices):
        for device in devices:
            copies.remote(tail, tail, rt, device)

    pl.when(later & jnp.logical_not(last))(lambda: copies.arrived(tail, rt))
    ahead = [at(to_x, z, 0) for to_x in range(edge)]
    copies.group(later & last, lambda: hand_out([over[0], *ahead, *over[1:], at(x, z, 1)]))
    copies.group(
        later & led & (x == 0), lambda: hand_out([at(edge, z, 0), at(edge, z, 1)])
    )
    copies.group(
        later & (core == 0) & (x != edge), lambda: hand_out([at(x, z, 1)])
    )
    dloc[...] += dot3(split(gain[...]), split(tail[...]))
    copies.group(home, lambda: copies.local(dloc, solved, lx.at[pairs]))
    copies.group(away, lambda: copies.remote(dloc, solved, rx.at[pairs], partner))

    @pl.when(away)
    def _():
        for m in range(pairs):
            result = inv.at[:, pl.ds(m * wide, wide)]
            pl.when(mine >= m)(lambda m=m, result=result: copies.arrived(result, rx.at[m]))
        copies.arrived(solved, rx.at[pairs])

    copies.finish()


def invert(factor, coupling, right_side):
    size, order = factor.shape
    columns, width = right_side.shape[1], coupling.shape[0]
    planes = lax.axis_size("blk") // 2
    pairs, wide = order // (2 * size), 2 * size
    vmem = pl.BlockSpec(memory_space=pltpu.VMEM)
    hbm = pl.BlockSpec(memory_space=pl.ANY)
    dma = pltpu.SemaphoreType.DMA
    panels = 2 * pairs
    return pl.pallas_call(
        functools.partial(solve_kernel, pairs, planes),
        out_shape=(
            jax.ShapeDtypeStruct((size, order), jnp.float32),
            jax.ShapeDtypeStruct((size, columns), jnp.float32),
        ),
        in_specs=[hbm, vmem, vmem],
        out_specs=(hbm, hbm),
        scratch_shapes=[
            *[pltpu.VMEM((wide, wide * m), jnp.float32) for m in range(1, pairs)],
            pltpu.VMEM((order, wide + columns), jnp.float32),
            pltpu.VMEM((size, wide + columns), jnp.float32),
            pltpu.VMEM((size, order), jnp.float32),
            pltpu.VMEM((size, size), jnp.float32),
            pltpu.VMEM((size, size), jnp.float32),
            pltpu.VMEM((size, columns), jnp.float32),
            pltpu.VMEM((2, size, wide), jnp.bfloat16),
            pltpu.VMEM((width, width), jnp.float32),
            pltpu.VMEM((size, width), jnp.float32),
            pltpu.VMEM((2, width, width + columns), jnp.float32),
            pltpu.VMEM((width, width + columns), jnp.float32),
            pltpu.VMEM((planes, width, width + columns), jnp.float32),
            pltpu.VMEM((width, columns), jnp.float32),
            pltpu.VMEM((size, wide), jnp.float32),
            dma((400,)),
            dma((panels, 2)),
            dma((panels, 2)),
            dma((pairs + 1,)),
            dma,
            dma((pairs + 1,)),
            dma,
            dma,
            dma((planes,)),
            dma,
            dma,
        ],
        compiler_params=pltpu.CompilerParams(
            collective_id=0, has_side_effects=True, vmem_limit_bytes=52 * 1024 * 1024
        ),
    )(factor, right_side, coupling)


def on_device(factor, coupling, right_side):
    inverse, solved = invert(factor[0], coupling[0], right_side[0])
    return inverse[None], solved[None]


def solution(mesh):
    in_specs = (P("blk", "row", None), P("blk", None, None), P("blk", "row", None))
    out_specs = (P("blk", "row", None), P("blk", "row", None))
    return jax.shard_map(
        on_device, mesh=mesh, in_specs=in_specs, out_specs=out_specs, check_vma=False
    )
```

```python
import functools

import jax
import jax.numpy as jnp
from jax import lax
from jax.experimental import pallas as pl
from jax.experimental.pallas import tpu as pltpu
from jax.sharding import PartitionSpec as P

MESH = pl.DeviceIdType.MESH
RING = 4
TARGETS = {0: (3, 1, 2), 1: (0, 2), 2: (3,), 3: ()}
TURNED = (2,)
RELAYED = {1: (3,)}


def dot(a, b):
    return jnp.dot(a, b, precision=lax.Precision.HIGHEST, preferred_element_type=jnp.float32)


def split(a):
    high = a.astype(jnp.bfloat16)
    return high, (a - high.astype(jnp.float32)).astype(jnp.bfloat16)


def dot3(a, b):
    (a_high, a_low), (b_high, b_low) = a, b

    def one(p, q):
        return jnp.dot(p, q, preferred_element_type=jnp.float32)

    return one(a_high, b_high) + (one(a_high, b_low) + one(a_low, b_high))


def unit_lower_inverse(matrix):
    size = matrix.shape[0]
    rows = lax.broadcasted_iota(jnp.int32, (size, size), 0)
    cols = lax.broadcasted_iota(jnp.int32, (size, size), 1)
    inverse = jnp.where(rows == cols, 1.0, 0.0).astype(jnp.float32)
    bit = 0
    while (1 << bit) < size:
        same = (rows >> (bit + 1)) == (cols >> (bit + 1))
        corner = same & (((rows >> bit) & 1) == 1) & (((cols >> bit) & 1) == 0)
        below = jnp.where(corner, matrix, 0.0)
        if bit == 0:
            inverse = inverse - below
        else:
            inverse = inverse - dot(dot(inverse, below), inverse)
        bit += 1
    return inverse


class Copies:
    def __init__(self, sems):
        self.sems, self.used, self.groups, self.depth, self.ending = sems, 0, [], 0, False

    def slot(self):
        self.used += 1
        return self.used - 1

    def group(self, when, body):
        if not self.depth and not self.ending:
            self.groups.append((when, body, self.used))
        self.depth += 1
        pl.when(when)(lambda: body())
        self.depth -= 1

    def arrived(self, target, sem):
        if not self.ending:
            pltpu.make_async_copy(target, target, sem).wait()

    def remote(self, source, target, arrival, device, slot=None):
        copy = pltpu.make_async_remote_copy(
            src_ref=source,
            dst_ref=target,
            send_sem=self.sems.at[self.slot() if slot is None else slot],
            recv_sem=arrival,
            device_id=device,
            device_id_type=MESH,
        )
        if self.ending:
            copy.wait_send()
        else:
            copy.start()

    def local(self, source, target, sem, waited=True):
        copy = pltpu.make_async_copy(source, target, sem)
        if not self.ending:
            copy.start()
        elif waited:
            copy.wait()

    def finish(self):
        self.ending = True
        for when, body, self.used in self.groups:
            self.group(when, body)


def solve_kernel(pairs, planes, fac, rhs, coupling, inv, solved, *scratch):
    lbuf = (None, *scratch[: pairs - 1])
    ebuf, own, xa, dinv, dleft, dloc, parts, cpl, gain, maps, mine_map, joined, tail, frames = scratch[
        pairs - 1 : pairs + 13
    ]
    sends, rl, re, rx, rd, lx, rc, rp, rj, rt, lf = scratch[pairs + 13 :]
    size = fac.shape[0]
    half, wide = size // 2, 2 * size
    lead, unit = rhs.shape[1], min(128, size)
    widths = (lead + -(-size // unit) * unit, lead + wide)
    blk, row = lax.axis_index("blk"), lax.axis_index("row")
    core = lax.rem(blk, 2)
    x, z = lax.div(row, RING), lax.rem(row, RING)
    zhi, odd = lax.div(z, 2), lax.rem(z, 2)
    mine = 2 * x + zhi
    home = core == 1 - odd
    away = core == odd
    first = blk - core

    def at(to_x, to_z, to_core):
        return {"blk": first + to_core, "row": to_x * RING + to_z}

    def aligned(index, by):
        return pl.multiple_of(index, by)

    barrier = pltpu.get_barrier_semaphore()
    peers = [(x, z, 1 - core)]
    for step in range(1, RING):
        for side in range(2):
            peers += [(x, lax.rem(z + step, RING), side), (lax.rem(x + step, RING), z, side)]
    others = [
        {"blk": lax.rem(blk + 2 * step, 2 * planes), "row": row} for step in range(1, planes)
    ]
    peers = [at(*peer) for peer in peers] + others
    for peer in peers:
        pl.semaphore_signal(barrier, inc=1, device_id=peer, device_id_type=MESH)

    edge = RING - 1
    row_lead = (zhi == 1) & (core == 0)
    last = row_lead & (x == edge)
    led = (zhi == 0) & (core == 0) & (x != edge)
    over = [at(to_x, lax.rem(z + 2, RING), 0) for to_x in range(edge)]

    @pl.when(last)
    def _():
        for peer in over:
            pl.semaphore_signal(barrier, inc=1, device_id=peer, device_id_type=MESH)

    @pl.when(led)
    def _():
        lead_of = at(edge, lax.rem(z + 2, RING), 0)
        pl.semaphore_signal(barrier, inc=1, device_id=lead_of, device_id_type=MESH)

    xa[...] = jnp.zeros_like(xa)
    dloc[...] = jnp.zeros_like(dloc)
    for m in range(pairs):
        rest = pl.ds(widths[0], widths[1] - widths[0])
        ebuf[pl.ds(m * wide, size), rest] = jnp.zeros((size, widths[1] - widths[0]), jnp.float32)
    part_of = pltpu.make_async_copy(fac.at[:, pl.ds(aligned(mine * wide, wide), wide)], frames, lf)
    part_of.start()
    part_of.wait()
    frame = frames[...]
    turned = pltpu.roll(frame, size, 1)
    dinv[...] = unit_lower_inverse(jnp.where(odd == 1, turned, frame)[:, :size])
    r_ids = lax.broadcasted_iota(jnp.int32, (size, wide), 0)
    c_ids = lax.broadcasted_iota(jnp.int32, (size, wide), 1)
    place = jnp.where(c_ids == r_ids + odd * size, 1.0, 0.0).astype(jnp.float32)
    own[:, pl.ds(lead, wide)] = dot(dinv[...], place)
    own[:, pl.ds(0, lead)] = rhs[...]
    before = dot(dinv[...], frames[:, :size])
    extra = jnp.where(last, len(over), jnp.where(led, 1, 0))
    pl.semaphore_wait(barrier, len(peers) + extra)

    copies = Copies(sends)
    beside = at(x, z + 1 - 2 * odd, core)

    def share_coupling():
        copies.local(coupling, cpl, rc, waited=False)
        copies.remote(coupling, cpl, rc, at(x, z, 1 - core))

    copies.group(home, share_coupling)
    copies.group(odd == 0, lambda: copies.remote(dinv, dleft, rd, beside))

    def near(source, target, arrival, slots):
        sides = [(source(side), target(side), arrival.at[row, side], side) for side in range(2)]

        def at_home():
            for src, dst, sem, side in sides:
                copies.remote(src, dst, sem, at(x, z, 1 - core), slots[side])
                copies.local(src, dst, sem, waited=False)

        def along(targets):
            for number, to_x in enumerate(targets):
                for src, dst, sem, side in sides:
                    copies.remote(src, dst, sem, at(to_x, z, side), slots[2 * number + 2 + side])

        copies.group(home, at_home)
        for r, targets in TARGETS.items():
            if targets:
                copies.group(home & (x == r), functools.partial(along, targets))
        for number, step in enumerate((1, 3)):
            to_z = lax.rem(z + step, RING)

            def beside(number=number, to_z=to_z):
                for src, dst, sem, side in sides:
                    copies.remote(src, dst, sem, at(x, to_z, side), slots[2 * number + side])

            copies.group(away & wanted(to_z), beside)

    def far(source, target, arrival, slots):
        to_z = lax.rem(z + 2, RING)

        def across():
            for side in range(2):
                copies.remote(
                    source(side), target(side), arrival.at[row, side], at(x, to_z, side), slots[side]
                )

        copies.group(home & wanted(to_z), across)

    def wanted(to_z):
        return (x < RING - 1) | (zhi == 0) | (lax.div(to_z, 2) == 1)

    def own_left(how, slots, numbers):
        for m in numbers:
            if m == 0:
                continue
            copies.group(
                mine == m,
                lambda m=m: how(
                    lambda side: fac.at[pl.ds(side * half, half), pl.ds(0, wide * m)],
                    lambda side: lbuf[m].at[pl.ds(aligned(odd * size + side * half, 8), half), :],
                    rl,
                    slots,
                ),
            )

    def own_right(how, slots):
        for parity, width in enumerate(widths):
            cols = pl.ds(0, width)
            copies.group(
                odd == parity,
                lambda cols=cols: how(
                    lambda side: own.at[pl.ds(side * half, half), cols],
                    lambda side: ebuf.at[pl.ds(aligned(row * size + side * half, 8), half), cols],
                    re,
                    slots,
                ),
            )

    slots = [copies.slot() for _ in range(8)]
    own_left(near, slots, range(pairs))
    farther = [copies.slot() for _ in range(4)]

    @pl.when(odd == 1)
    def _():
        pltpu.make_async_copy(dleft, dleft, rd).wait()
        left = dot(before, dleft[...])
        front = jnp.where(c_ids == r_ids, 1.0, 0.0).astype(jnp.float32)
        own[:, pl.ds(lead, wide)] = own[:, pl.ds(lead, wide)] - dot(left, front)

    slots = [copies.slot() for _ in range(8)]
    own_right(near, slots)

    def view(kind, j, side):
        if kind == "left":
            return lbuf[j // 2].at[pl.ds(aligned((j % 2) * size + side * half, 8), half), :]
        cols = pl.ds(0, widths[j % 2])
        return ebuf.at[pl.ds(aligned(j * size + side * half, 8), half), cols]

    def sem_of(kind, j, side):
        return (rl if kind == "left" else re).at[j, side]

    def panels(kind, numbers):
        return [j for j in numbers if kind == "right" or j >= 2]

    def forward(kind, j, when, targets, beside_too, across=False):
        here, sem = view(kind, j, core), sem_of(kind, j, core)

        def pass_on():
            copies.arrived(here, sem)
            for to_x in targets:
                copies.remote(here, here, sem, at(to_x, z, core))
            if across:
                copies.remote(here, here, sem, at(x, lax.rem(z + 2, RING), core))
            if beside_too is not None:
                copies.group(
                    beside_too, lambda: copies.remote(here, here, sem, at(x, z, 1 - core))
                )

        copies.group(when, pass_on)

    def row_pass(kind, r, hops, targets, beside_too=True):
        for j in panels(kind, range(RING * r, RING * (r + 1))):
            apart = lax.rem(z + RING - j % RING, RING)
            when = lax.rem(apart, 2) == 1 if hops == 1 else apart == hops
            if r == RING - 1 and j % RING >= 2:
                when = when & (zhi == 1)
            forward(kind, j, when, targets, (mine >= j // 2) if beside_too else None)

    def turn(kind, r):
        for q in TURNED:
            if q + 1 == r:
                for j in panels(kind, range(RING * q, RING * (q + 1))):
                    forward(kind, j, z == j % RING, (), mine >= j // 2, across=True)

    for r in range(RING):

        def own_row(r=r):
            relays = [(kind, q, RELAYED[q]) for q in RELAYED for kind in ("left", "right") if r == 0]

            def relay(kind, hops):
                for name, q, targets in relays:
                    if name == kind:
                        row_pass(kind, q, hops, targets, False)

            row_pass("left", r, 1, TARGETS[r])
            own_left(far, farther[:2], (2 * r, 2 * r + 1))
            turn("left", r)
            relay("left", 0)
            row_pass("right", r, 1, TARGETS[r])
            own_right(far, farther[2:])
            turn("right", r)
            relay("left", 1)
            onward = () if r in TURNED else TARGETS[r]
            row_pass("left", r, 2, onward)
            row_pass("right", r, 2, onward)
            relay("left", 2)
            for hops in range(3):
                relay("right", hops)

        copies.group(x == r, own_row)

    def take(m):
        def body():
            for kind in ("left", "right"):
                for j in panels(kind, (2 * m, 2 * m + 1)):
                    when = (z != j % RING) if m // 2 in TURNED else True
                    forward(kind, j, when, (), True)

        copies.group(x > m // 2, body)

    partner = at(x, z + 1 - 2 * odd, 1 - core)
    half_of_pair = jnp.where(home, odd, 1 - odd)

    def solve(m):
        here = mine >= m

        def wait():
            for kind in ("left", "right"):
                for j in panels(kind, (2 * m, 2 * m + 1)):
                    pl.when(row == j)(
                        lambda kind=kind, j=j: copies.arrived(view(kind, j, core), sem_of(kind, j, core))
                    )
                    copies.arrived(view(kind, j, 1 - core), sem_of(kind, j, 1 - core))

        pl.when(here)(wait)
        block = xa.at[:, pl.ds(m * wide, wide)]

        @pl.when(mine == m)
        def _():
            rows = pl.ds(aligned(m * wide + half_of_pair * size, 8), size)
            block[...] = ebuf[rows, pl.ds(lead, wide)]

        @pl.when(mine > m)
        def _():
            block[...] = dot3(split(block[...]), split(ebuf[pl.ds(m * wide, wide), pl.ds(lead, wide)]))

        @pl.when(here)
        def _():
            solved = split(block[...])
            dloc[...] += dot3(
                solved, split(ebuf[pl.ds(m * wide, wide), pl.ds(0, lead)])
            )
            parts[0, :, :], parts[1, :, :] = solved
            if m:

                @pl.loop(0, m)
                def _(n):
                    cols = pl.ds(pl.multiple_of(n * wide, wide), wide)
                    xa[:, cols] -= dot3((parts[0], parts[1]), split(lbuf[m][:, cols]))

        result = inv.at[:, pl.ds(m * wide, wide)]
        copies.group((mine < m) | home, lambda: copies.local(block, result, lx.at[m]))
        when = here & away
        if m < pairs // 2:
            when = when & jnp.logical_not(last)
        copies.group(when, lambda: copies.remote(block, result, rx.at[m], partner))

    for m in reversed(range(pairs)):
        solve(m)
        if 2 <= m:
            take(m - 2)
    width, columns = cpl.shape[0], dloc.shape[1]
    plane, which = lax.div(blk, 2), 1 - odd
    later = (plane > 0) | (which > 0)
    copies.arrived(cpl, rc)
    gain[...] = -dot3(split(xa[:, pl.ds(0, width)]), split(cpl[...]))

    @pl.when(last | jnp.logical_not(later))
    def _():
        tail[...] = jnp.zeros_like(tail)

    @pl.when(last)
    def _():
        maps[which, :, pl.ds(0, width)] = gain[pl.ds(size - width, width), :]
        maps[which, :, pl.ds(width, columns)] = dloc[pl.ds(size - width, width), :]

    copies.group(last, lambda: copies.remote(maps.at[which], maps.at[which], rp, beside))

    def held_back():
        for m in reversed(range(pairs // 2)):
            cols = pl.ds(m * wide, wide)
            copies.remote(xa.at[:, cols], inv.at[:, cols], rx.at[m], partner)

    copies.group(last & away, held_back)

    @pl.when(last)
    def _():
        copies.arrived(maps.at[1 - which], rp)
        mine_map[...] = dot3(split(maps[1, :, pl.ds(0, width)]), split(maps[0, :, :]))
        mine_map[:, pl.ds(width, columns)] += maps[1, :, pl.ds(width, columns)]

    for step, device in enumerate(others):
        copies.group(
            last & (plane + step + 1 < planes),
            lambda device=device: copies.remote(
                mine_map, joined.at[plane], rj.at[plane], device
            ),
        )

    def step_on(matrix_and_term):
        left = matrix_and_term[:, pl.ds(0, width)]
        tail[...] = dot3(split(left), split(tail[...])) + matrix_and_term[:, pl.ds(width, columns)]

    for k in range(planes - 1):

        @pl.when(last & (plane > k))
        def _():
            copies.arrived(joined.at[k], rj.at[k])
            step_on(joined.at[k])

    @pl.when(last & (which == 1))
    def _():
        step_on(maps.at[0])

    def hand_out(devices):
        for device in devices:
            copies.remote(tail, tail, rt, device)

    pl.when(later & jnp.logical_not(last))(lambda: copies.arrived(tail, rt))
    ahead = [at(to_x, z, 0) for to_x in range(edge)]
    copies.group(later & last, lambda: hand_out([over[0], *ahead, *over[1:], at(x, z, 1)]))
    copies.group(
        later & led & (x == 0), lambda: hand_out([at(edge, z, 0), at(edge, z, 1)])
    )
    copies.group(
        later & (core == 0) & (x != edge), lambda: hand_out([at(x, z, 1)])
    )
    dloc[...] += dot3(split(gain[...]), split(tail[...]))
    copies.group(home, lambda: copies.local(dloc, solved, lx.at[pairs]))
    copies.group(away, lambda: copies.remote(dloc, solved, rx.at[pairs], partner))

    @pl.when(away)
    def _():
        for m in range(pairs):
            result = inv.at[:, pl.ds(m * wide, wide)]
            pl.when(mine >= m)(lambda m=m, result=result: copies.arrived(result, rx.at[m]))
        copies.arrived(solved, rx.at[pairs])

    copies.finish()


def invert(factor, coupling, right_side):
    size, order = factor.shape
    columns, width = right_side.shape[1], coupling.shape[0]
    planes = lax.axis_size("blk") // 2
    pairs, wide = order // (2 * size), 2 * size
    vmem = pl.BlockSpec(memory_space=pltpu.VMEM)
    hbm = pl.BlockSpec(memory_space=pl.ANY)
    dma = pltpu.SemaphoreType.DMA
    panels = 2 * pairs
    return pl.pallas_call(
        functools.partial(solve_kernel, pairs, planes),
        out_shape=(
            jax.ShapeDtypeStruct((size, order), jnp.float32),
            jax.ShapeDtypeStruct((size, columns), jnp.float32),
        ),
        in_specs=[hbm, vmem, vmem],
        out_specs=(hbm, hbm),
        scratch_shapes=[
            *[pltpu.VMEM((wide, wide * m), jnp.float32) for m in range(1, pairs)],
            pltpu.VMEM((order, wide + columns), jnp.float32),
            pltpu.VMEM((size, wide + columns), jnp.float32),
            pltpu.VMEM((size, order), jnp.float32),
            pltpu.VMEM((size, size), jnp.float32),
            pltpu.VMEM((size, size), jnp.float32),
            pltpu.VMEM((size, columns), jnp.float32),
            pltpu.VMEM((2, size, wide), jnp.bfloat16),
            pltpu.VMEM((width, width), jnp.float32),
            pltpu.VMEM((size, width), jnp.float32),
            pltpu.VMEM((2, width, width + columns), jnp.float32),
            pltpu.VMEM((width, width + columns), jnp.float32),
            pltpu.VMEM((planes, width, width + columns), jnp.float32),
            pltpu.VMEM((width, columns), jnp.float32),
            pltpu.VMEM((size, wide), jnp.float32),
            dma((400,)),
            dma((panels, 2)),
            dma((panels, 2)),
            dma((pairs + 1,)),
            dma,
            dma((pairs + 1,)),
            dma,
            dma,
            dma((planes,)),
            dma,
            dma,
        ],
        compiler_params=pltpu.CompilerParams(
            collective_id=0, has_side_effects=True, vmem_limit_bytes=52 * 1024 * 1024
        ),
    )(factor, right_side, coupling)


def on_device(factor, coupling, right_side):
    inverse, solved = invert(factor[0], coupling[0], right_side[0])
    return inverse[None], solved[None]


def solution(mesh):
    in_specs = (P("blk", "row", None), P("blk", None, None), P("blk", "row", None))
    out_specs = (P("blk", "row", None), P("blk", "row", None))
    return jax.shard_map(
        on_device, mesh=mesh, in_specs=in_specs, out_specs=out_specs, check_vma=False
    )
```
